128 devices in a mesh: gx: 16 (over y, z), gy: 8 (over x, core).
Axes of the slice: x: 4, y: 4, z: 4, core: 2. Of those that a mesh axis runs over, the one named last changes fastest.
Arguments:
- temper_start: float32 [512, 512, 256], P('gx', 'gy'), may hold values from -4 to 4
- cure_start: float32 [512, 512, 256], P('gx', 'gy'), may hold values from 0.05 to 0.9
- temper_middle: float32 [512, 512, 256], P('gx', 'gy'), may hold values from -4 to 4
- cure_middle: float32 [512, 512, 256], P('gx', 'gy'), may hold values from 0.05 to 0.9
- adjoint_temper: float32 [512, 512, 256], P('gx', 'gy'), may hold values from -6 to 6
- adjoint_cure: float32 [512, 512, 256], P('gx', 'gy'), may hold values from -6 to 6
- conduct_first: float32 [528], P('gx'), may hold values from 0 to 3000, as said below
- inverse_first: float32 [512, 32], P('gx'), may hold values from 0 to 1, as said below
- conduct_second: float32 [520], P('gy'), may hold values from 0 to 3000, as said below
- inverse_second: float32 [512, 64], P('gy'), may hold values from 0 to 1, as said below
- conduct_thick: float32 [257], replicated, may hold values from 20 to 120
- inverse_thick: float32 [256, 256], replicated, may hold values from 0 to 1, as said below
Outputs:
- sensitivity_temper: float32 [512, 512, 256], P('gx', 'gy')
- sensitivity_cure: float32 [512, 512, 256], P('gx', 'gy')
The draws below stay inside these ranges and needn't reach their ends.
Inputs may be any that keep to these rules, and one draw needn't show every extreme that they name: `conduct_first`: group j of 33 entries holds the left faces of its 32 cells and then the face beyond them; entry 32 of group j equals entry 0 of group j + 1, and the last group's entry 32 is 0 (insulated side). `inverse_first`: rows j * 32 to (j + 1) * 32 - 1 are the inverse of group j's diagonal block of I + Kx restricted to that group: diagonal 1 plus the cell's two faces, off-diagonals minus the faces between its cells. `conduct_second`: group j of 65 entries holds the left faces of its 64 cells and then the face beyond them; entry 64 of group j equals entry 0 of group j + 1, and the last group's entry 64 is 0 (insulated side). `inverse_second`: rows j * 64 to (j + 1) * 64 - 1 are the inverse of group j's diagonal block of I + Ky restricted to that group. `inverse_thick`: the inverse of I + Kz through the thickness.
All inputs are finite; a program needn't handle non-finite values.
Results may differ from the reference program's by a relative error of at most 0.0003.
Values sent between devices are 32-bit elements; how exact they have to be, the bound alone decides.
No kernel may reach another device: no remote copies, remote signals or barrier semaphores. Data moves between devices by JAX's collectives and lax.ppermute only.
A program may use at most 128 MiB of HBM per device.

```python
import jax
import jax.numpy as jnp
from jax import lax

CX = 32
CY = 64
NZ = 256
NX = 512
NY = 512


def group_system(key, groups, width, insulated, shown_low, shown_high):
    total = groups * width
    logs = jax.random.uniform(key, (total + 1,), jnp.float32, jnp.log(shown_low), jnp.log(shown_high))
    raw = jnp.exp(logs)
    if insulated:
        raw = jnp.where(jnp.arange(total + 1) == total, 0.0, raw)
    positions = jnp.arange(groups)[:, None] * width + jnp.arange(width + 1)[None, :]
    faces = raw[positions]
    diagonal = 1.0 + faces[:, :-1] + faces[:, 1:]
    inner = -faces[:, 1:-1]
    zero_column = jnp.zeros((groups, 1), jnp.float32)
    below = jnp.concatenate([zero_column, inner], axis=1)
    above = jnp.concatenate([inner, zero_column], axis=1)
    identity = jnp.broadcast_to(jnp.eye(width, dtype=jnp.float32), (groups, width, width))
    inverse = lax.linalg.tridiagonal_solve(below, diagonal, above, identity)
    return (faces.reshape(-1), inverse.reshape(total, width))


def draw_conduct_first(key, part):
    return group_system(jax.random.fold_in(key, 101), NX // CX, CX, True, 400.0, 2500.0)[0]


def draw_inverse_first(key, part):
    return group_system(jax.random.fold_in(key, 101), NX // CX, CX, True, 400.0, 2500.0)[1]


def draw_conduct_second(key, part):
    return group_system(jax.random.fold_in(key, 202), NY // CY, CY, True, 400.0, 2500.0)[0]


def draw_inverse_second(key, part):
    return group_system(jax.random.fold_in(key, 202), NY // CY, CY, True, 400.0, 2500.0)[1]


def draw_conduct_thick(key, part):
    return group_system(jax.random.fold_in(key, 303), 1, NZ, False, 30.0, 80.0)[0]


def draw_inverse_thick(key, part):
    return group_system(jax.random.fold_in(key, 303), 1, NZ, False, 30.0, 80.0)[1]


def level_of(stream_key, extent, pieces, least, largest):
    gain = 1.0
    for position, blocks in pieces:
        heights = jax.random.uniform(jax.random.fold_in(jax.random.fold_in(stream_key, 6), position), (blocks,), jnp.float32, least / len(pieces), largest / len(pieces))
        gain = gain * jnp.repeat(jnp.exp(heights), extent[position] // blocks).reshape((-1,) + (1,) * (len(extent) - 1 - position))
    return gain


def centred(key, extent, spread, reach, shards=(), kind=jnp.bfloat16):
    entries = spread * jax.random.normal(key, extent, jnp.float32)
    if shards:
        entries = entries * level_of(key, extent, shards, -0.22, 0.18)
    return jnp.clip(entries, -reach, reach).astype(kind)


def setup_inputs(seed: int = 0) -> dict:
    key_of = jax.random.split(jax.random.key(seed), 13)
    return {
        "temper_start": centred(key_of[0], (NX, NY, NZ), 0.8, 4.0, ((0, 16), (1, 8)), jnp.float32),
        "cure_start": jnp.clip(0.05 + 0.84999998 * jax.random.uniform(key_of[1], (NX, NY, NZ), jnp.float32) ** level_of(key_of[1], (NX, NY, NZ), ((0, 16), (1, 8)), -0.2, 0.2), 0.05, 0.9),
        "temper_middle": centred(key_of[2], (NX, NY, NZ), 0.8, 4.0, ((0, 16), (1, 8)), jnp.float32),
        "cure_middle": jnp.clip(0.05 + 0.84999998 * jax.random.uniform(key_of[3], (NX, NY, NZ), jnp.float32) ** level_of(key_of[3], (NX, NY, NZ), ((0, 16), (1, 8)), -0.2, 0.2), 0.05, 0.9),
        "adjoint_temper": centred(key_of[4], (NX, NY, NZ), 1.0, 6.0, ((0, 16), (1, 8)), jnp.float32),
        "adjoint_cure": centred(key_of[5], (NX, NY, NZ), 1.0, 6.0, ((0, 16), (1, 8)), jnp.float32),
        "conduct_first": draw_conduct_first(jax.random.fold_in(key_of[12], 71), 0),
        "inverse_first": draw_inverse_first(jax.random.fold_in(key_of[12], 71), 0),
        "conduct_second": draw_conduct_second(jax.random.fold_in(key_of[12], 71), 0),
        "inverse_second": draw_inverse_second(jax.random.fold_in(key_of[12], 71), 0),
        "conduct_thick": draw_conduct_thick(jax.random.fold_in(key_of[12], 71), 0),
        "inverse_thick": draw_inverse_thick(jax.random.fold_in(key_of[12], 71), 0),
    }


explicit_part = 2.0
heat_release = 100.0
cure_step = 0.5
arrhenius = 0.5
initial_rate = 0.1
highest = lax.Precision.HIGHEST

def reduced_solve(first_tip, last_tip, spike_ends):
    empty_row = jnp.zeros_like(first_tip[:1])

    def forward(running, inputs):
        corner_prev, partial_prev = running
        tail_here, head_next, left_here, right_here, value_last, value_first = inputs
        upper_entry = -tail_here - left_here * right_here * corner_prev
        lower_entry = -head_next
        determinant = 1.0 - upper_entry * lower_entry
        corner = -upper_entry / determinant
        bottom = 1.0 / determinant
        shifted = value_last + left_here * partial_prev
        solved_top = bottom * shifted + corner * value_first
        solved_low = -lower_entry / determinant * shifted + bottom * value_first
        return ((corner, solved_top), (solved_top, solved_low, corner, bottom))
    start_state = (jnp.zeros((), jnp.float32), jnp.zeros_like(first_tip[0]))
    inputs = (spike_ends[:-1, 3], spike_ends[1:, 0], spike_ends[:-1, 1], spike_ends[:-1, 2], last_tip[:-1], first_tip[1:])
    unused, (tops, lows, corners, bottoms) = lax.scan(forward, start_state, inputs)

    def backward(next_low, inputs):
        solved_top, solved_low, corner, bottom, right_next = inputs
        top_value = solved_top + corner * right_next * next_low
        low_value = solved_low + bottom * right_next * next_low
        return (low_value, (top_value, low_value))
    unused, (top_values, low_values) = lax.scan(backward, jnp.zeros_like(first_tip[0]), (tops, lows, corners, bottoms, spike_ends[1:, 2]), reverse=True)
    next_first = jnp.concatenate([low_values, empty_row], axis=0)
    prev_last = jnp.concatenate([empty_row, top_values], axis=0)
    return (next_first, prev_last)

def group_solve(right_side, inverse, faces, width):
    groups = right_side.shape[0] // width
    blocks = inverse.reshape(groups, width, width)
    blockwise = jnp.einsum('jba,jbl->jal', blocks, right_side.reshape(groups, width, -1), precision=highest)
    edges = faces.reshape(groups, width + 1)
    left_spike = edges[:, :1] * blocks[:, 0, :]
    right_spike = edges[:, width:] * blocks[:, width - 1, :]
    spike_ends = jnp.stack([left_spike[:, 0], left_spike[:, -1], right_spike[:, 0], right_spike[:, -1]], axis=1)
    next_first, prev_last = reduced_solve(blockwise[:, 0], blockwise[:, -1], spike_ends)
    result = blockwise + left_spike[:, :, None] * prev_last[:, None, :] + right_spike[:, :, None] * next_first[:, None, :]
    return result.reshape(groups * width, -1)

def along_axis(values, faces, width, axis):
    moved = jnp.moveaxis(values, axis, 0)
    length = moved.shape[0]
    edges = faces.reshape(-1, width + 1)
    left_face = edges[:, :width].reshape(length)[:, None, None]
    right_face = edges[:, 1:].reshape(length)[:, None, None]
    zero_layer = jnp.zeros_like(moved[:1])
    below = jnp.concatenate([zero_layer, moved[:-1]], axis=0)
    above = jnp.concatenate([moved[1:], zero_layer], axis=0)
    term = left_face * (moved - below) + right_face * (moved - above)
    return jnp.moveaxis(term, 0, axis)

def stiffness(field, conduct_first, conduct_second, conduct_thick):
    total = along_axis(field, conduct_first, CX, 0)
    total = total + along_axis(field, conduct_second, CY, 1)
    return total + along_axis(field, conduct_thick, NZ, 2)

def reference(temper_start, cure_start, temper_middle, cure_middle, adjoint_temper, adjoint_cure, conduct_first, inverse_first, conduct_second, inverse_second, conduct_thick, inverse_thick):
    temp_adjoint = adjoint_temper
    cure_adjoint = adjoint_cure
    for temper, cure in ((temper_middle, cure_middle), (temper_start, cure_start)):
        heating = jnp.exp(arrhenius * temper)
        remain = 1.0 - cure
        rate = heating * (initial_rate + cure) * remain * remain
        rate_temp = arrhenius * rate
        rate_cure = heating * (remain * remain - 2.0 * (initial_rate + cure) * remain)
        size_a, size_b, size_c = temp_adjoint.shape
        through = jnp.dot(temp_adjoint.reshape(-1, size_c), inverse_thick, precision=highest).reshape(size_a, size_b, size_c)
        moved = jnp.moveaxis(through, 1, 0).reshape(size_b, -1)
        second_done = group_solve(moved, inverse_second, conduct_second, CY).reshape(size_b, size_a, size_c)
        second_done = jnp.moveaxis(second_done, 0, 1)
        adjoint_flux = group_solve(second_done.reshape(size_a, -1), inverse_first, conduct_first, CX).reshape(size_a, size_b, size_c)
        source = heat_release * adjoint_flux + cure_step * cure_adjoint
        kick = stiffness(adjoint_flux, conduct_first, conduct_second, conduct_thick)
        temp_adjoint = temp_adjoint - explicit_part * kick + rate_temp * source
        cure_adjoint = cure_adjoint + rate_cure * source
    return (temp_adjoint, cure_adjoint)
```

```python
import functools

import jax
import jax.numpy as jnp
from jax import lax
from jax.experimental import pallas as pl
from jax.experimental.pallas import tpu as pltpu
from jax.sharding import PartitionSpec as P

explicit_part = 2.0
heat_release = 100.0
cure_step = 0.5
arrhenius = 0.5
initial_rate = 0.1
highest = lax.Precision.HIGHEST

NX, NY, NZ = 32, 64, 256
ROWS_X, ROWS_Y = 72, 40
DATA_X, DATA_Y = 64, 34
MIB = 1024 * 1024


vmem = pl.BlockSpec(memory_space=pltpu.VMEM)
smem = pl.BlockSpec(memory_space=pltpu.SMEM)


def f32(*shape):
    return jax.ShapeDtypeStruct(shape, jnp.float32)


def bf16(*shape):
    return jax.ShapeDtypeStruct(shape, jnp.bfloat16)


def call(kernel, name, operands, in_specs, outs, scratch=(), flops=0, limit=12, out_space=vmem):
    size = sum(x.size * 4 for x in operands) + sum(o.size * 4 for o in outs)
    return pl.pallas_call(
        kernel,
        name=name,
        out_shape=tuple(outs),
        in_specs=list(in_specs),
        out_specs=tuple([out_space] * len(outs)),
        scratch_shapes=list(scratch),
        compiler_params=pltpu.CompilerParams(vmem_limit_bytes=limit * MIB),
        cost_estimate=pl.CostEstimate(flops=flops, bytes_accessed=size, transcendentals=0),
    )(*operands)


def chain(count, place, parts, data, gather, alphas, betas):
    rows = gather.shape[2]
    for shift, part in enumerate(parts):
        gather[lax.rem(place - shift + count, count)] = part[...]
    row = lax.broadcasted_iota(jnp.int32, (rows, NZ), 0)
    is_left, is_right = row == data, row == data + 1

    def source(j, end):
        value = gather[j, end]
        if j != 0:
            value = jnp.where(is_left, 0.0, value)
        if j != count - 1:
            value = jnp.where(is_right, 0.0, value)
        return value

    def coefficient(j, end, side):
        return gather[j, end, data + side : data + side + 1, :]

    first = [source(j, 0) for j in range(count)]
    last = [source(j, 1) for j in range(count)]
    left_first = [coefficient(j, 0, 0) for j in range(count)]
    left_last = [coefficient(j, 1, 0) for j in range(count)]
    right_first = [coefficient(j, 0, 1) for j in range(count)]
    right_last = [coefficient(j, 1, 1) for j in range(count)]

    pre, corner = [last[0]], [right_last[0]]
    for t in range(1, count):
        inv = 1.0 / (1.0 - corner[-1] * left_first[t])
        gain = left_last[t] * inv
        pre.append(last[t] + gain * (pre[-1] + corner[-1] * first[t]))
        corner.append(right_last[t] + gain * corner[-1] * right_first[t])
    post, bend = {count - 1: first[-1]}, {count - 1: left_first[-1]}
    for t in range(count - 2, -1, -1):
        e, g = post[t + 1], bend[t + 1]
        gain = right_first[t] / (1.0 - g * right_last[t])
        post[t] = first[t] + gain * (e + g * last[t])
        bend[t] = left_first[t] + gain * g * left_last[t]
    alphas[0] = jnp.where(is_left, 1.0, jnp.zeros((rows, NZ), jnp.float32))
    betas[count - 1] = jnp.where(is_right, 1.0, jnp.zeros((rows, NZ), jnp.float32))
    for t in range(count - 1):
        a, c, e, g = pre[t], corner[t], post[t + 1], bend[t + 1]
        inv = 1.0 / (1.0 - c * g)
        alphas[t + 1] = (a + c * e) * inv
        betas[t] = (e + g * a) * inv
    return post[0], pre[-1], alphas[place], betas[place]


def chain_scratch(count, rows):
    return [
        pltpu.VMEM((count, 2, rows, NZ), jnp.float32),
        pltpu.VMEM((count, rows, NZ), jnp.float32),
        pltpu.VMEM((count, rows, NZ), jnp.float32),
    ]


def end_rows(out, end, start, left, right):
    row = lax.broadcasted_iota(jnp.int32, (8, NZ), 0)
    block = jnp.where(row == 0, left, jnp.where(row == 1, right, 0.0))
    out[end, start : start + 8, :] = block


def tips_kernel(inv, faces, field, out):
    for block in range(4):
        span = slice(block * 16, block * 16 + 16)
        low = inv[0, 0] * field[0, span, :]
        high = inv[0, NX - 1] * field[0, span, :]
        for i in range(1, NX):
            value = field[i, span, :]
            low = low + inv[i, 0] * value
            high = high + inv[i, NX - 1] * value
        out[0, span, :] = low
        out[1, span, :] = high
    x_end_rows(out, inv, faces)


def x_end_rows(out, inv, faces):
    end_rows(out, 0, DATA_X, faces[0] * inv[0, 0], faces[NX] * inv[NX - 1, 0])
    end_rows(out, 1, DATA_X, faces[0] * inv[0, NX - 1], faces[NX] * inv[NX - 1, NX - 1])


def chain_kernel(count, data, place, *refs):
    parts, (tips, own), scratch = refs[:count], refs[count : count + 2], refs[count + 2 :]
    e, a, alpha, beta = chain(count, place[0], parts, data, *scratch)
    tips[0] = e
    tips[1] = a
    own[0] = alpha
    own[1] = beta


def split(value):
    high = value.astype(jnp.bfloat16)
    return high, (value - high.astype(jnp.float32)).astype(jnp.bfloat16)


def product(left, right):
    return jnp.dot(left, right, preferred_element_type=jnp.float32)


def times_thick(value, thick_high, thick_low):
    high, low = split(value)
    total = product(low, thick_high[...]) + product(high, thick_low[...])
    return total + product(high, thick_high[...])


def times_second(second, value):
    high, low = split(value)
    return product(second[...], jnp.concatenate([high, high, low], axis=0))


def prepare_kernel(
    inv, faces, inv_second, faces_second, inverse_thick, inverse_t, thick,
    table, spikes, thick_high, thick_low, second, thick_rows,
):
    def row(value):
        return jnp.full((1, NZ), value, jnp.float32)

    delta = row(1.0 + faces[0] + faces[1])
    for i in range(NX):
        table[0, i : i + 1, :] = row(faces[0] * inv[0, i])
        table[1, i : i + 1, :] = row(faces[NX] * inv[NX - 1, i])
        table[2, i : i + 1, :] = row(faces[i])
        table[3, i : i + 1, :] = row(faces[i + 1])
        inverse = 1.0 / delta
        table[5, i : i + 1, :] = inverse
        ratio = faces[i + 1] * inverse
        table[4, i : i + 1, :] = ratio
        if i < NX - 1:
            delta = 1.0 + faces[i + 1] + faces[i + 2] - faces[i + 1] * ratio
    for y in range(NY):
        spikes[0, y : y + 1, :] = row(faces_second[0] * inv_second[0, y])
        spikes[1, y : y + 1, :] = row(faces_second[NY] * inv_second[NY - 1, y])
    thick_high[...], thick_low[...] = split(inverse_thick[...])
    high, low = split(inverse_t[...])
    second[...] = jnp.concatenate([high, low, high], axis=1)
    below, above = thick[:, 0:NZ], thick[:, 1 : NZ + 1]
    lane = lax.broadcasted_iota(jnp.int32, (1, NZ), 1)
    thick_rows[0:1, :] = below
    thick_rows[1:2, :] = above
    thick_rows[2:3, :] = below + above
    thick_rows[3:4, :] = jnp.where(lane == 0, 0.0, below)
    thick_rows[4:5, :] = jnp.where(lane == NZ - 1, 0.0, above)


def rates_kernel(temper, cure, gain, cure_gain):
    @pl.loop(0, NX, unroll=2)
    def _(i):
        c = cure[i]
        heating = jnp.exp(arrhenius * temper[i])
        remain = 1.0 - c
        heated = heating * remain
        ready = initial_rate + c
        gain[i] = (heat_release * arrhenius) * (heated * ready * remain)
        cure_gain[i] = heat_release * (heated * (remain - 2.0 * ready))


def solve_z_kernel(field, thick_high, thick_low, out):
    @pl.loop(0, 8)
    def _(block):
        span = pl.ds(block * 4, 4)
        value = field[span].reshape(4 * NY, NZ)
        out[span] = times_thick(value, thick_high, thick_low).reshape(4, NY, NZ)


def solve_y_kernel(field, second, inv, out, tips, ends):
    @pl.loop(0, NX, unroll=4)
    def _(i):
        value = times_second(second, field[i])
        out[i] = value
        ends[0, pl.ds(i, 1), :] = value[0:1]
        ends[1, pl.ds(i, 1), :] = value[NY - 1 : NY]

    for end in range(2):
        tips[end] = lax.dot_general(
            inv[...],
            ends[end],
            (((0,), (0,)), ((), ())),
            precision=highest,
            preferred_element_type=jnp.float32,
        )


def middle_kernel(
    place, inv_second, faces_second, *refs
):
    parts = refs[:4]
    own, thick_high, thick_low, second_matrix, tips, table = refs[4:10]
    out, through, second = refs[10:13]
    scratch = refs[13:16]
    halo = refs[16]
    unused, unused, p, n = chain(4, place[0], parts, DATA_X, *scratch)
    p, n = p[:DATA_X], n[:DATA_X]
    for side in range(2):
        halo[side] = (
            own[side, :DATA_X, :]
            + own[side, DATA_X : DATA_X + 1, :] * p
            + own[side, DATA_X + 1 : DATA_X + 2, :] * n
        )
    through[...] = times_thick(
        halo[...].reshape(2 * NY, NZ), thick_high, thick_low
    ).reshape(2, NY, NZ)
    for side in range(2):
        second[side] = times_second(second_matrix, through[side])
    a, b = faces_second[0], faces_second[NY]
    for end in range(2):
        y = end * (NY - 1)
        prev_row, next_row = second[0, y : y + 1, :], second[1, y : y + 1, :]
        out[end, :NX, :] = tips[end] + table[0] * prev_row + table[1] * next_row
        row = lax.broadcasted_iota(jnp.int32, (8, NZ), 0)
        left, right = a * inv_second[0, y], b * inv_second[NY - 1, y]
        out[end, NX:, :] = jnp.where(
            row == 0,
            prev_row,
            jnp.where(row == 1, next_row, jnp.where(row == 2, left, jnp.where(row == 3, right, 0.0))),
        )


def lane_stencil(value, thick):
    lower, upper = pltpu.roll(value, 1, 1), pltpu.roll(value, NZ - 1, 1)
    return thick[2:3, :] * value - thick[3:4, :] * lower - thick[4:5, :] * upper


def local_kernel(
    faces, second_done, through, temp, cure_adj, gain, cure_gain, second, halo_through, table, thick,
    base, cure_base, work, work_through,
):
    for block in range(4):
        span = slice(block * 16, block * 16 + 16)

        def forward(i, carry):
            value, whole, ratio = carry
            value = second_done[i, span, :] + ratio * value
            whole = through[i, span, :] + ratio * whole
            work[i] = value
            work_through[i] = whole
            return value, whole, table[4, pl.ds(i, 1), :]

        start = (second[0, span, :], halo_through[0, span, :], table[2, 0:1, :])
        lax.fori_loop(0, NX, forward, start, unroll=4)

        def backward(step, carry):
            i = NX - 1 - step
            value, whole = carry
            inverse, ratio = table[5, pl.ds(i, 1), :], table[4, pl.ds(i, 1), :]
            value = inverse * work[i] + ratio * value
            whole = inverse * work_through[i] + ratio * whole
            kick = (second_done[i, span, :] - value) + (whole - value) + lane_stencil(value, thick)
            f, h, lc = gain[i, span, :], cure_gain[i, span, :], cure_adj[i, span, :]
            source = value + (cure_step / heat_release) * lc
            base[i, span, :] = temp[i, span, :] - explicit_part * kick + f * source
            cure_base[i, span, :] = lc + h * source
            return value, whole

        lax.fori_loop(
            0, NX, backward, (second[1, span, :], halo_through[1, span, :]), unroll=4
        )


def final_kernel(last, place, inv, faces, *refs):
    parts = refs[:4]
    own, base, gain, cure_base, cure_gain, spikes, table, thick = refs[4:12]
    outs = 2 if last else 3
    temp_out, cure_out = refs[12:14]
    rest = refs[12 + outs :]
    scratch, halo, kicks = rest[:3], rest[3], rest[4]
    unused, unused, p, n = chain(4, place[0], parts, DATA_Y, *scratch)
    for side in range(2):
        value = (
            own[side]
            + own[side, DATA_Y : DATA_Y + 1, :] * p
            + own[side, DATA_Y + 1 : DATA_Y + 2, :] * n
        )
        halo[side, 8:40, :] = value[:NX]
        halo[side, 7:8, :] = value[NX : NX + 1]
        halo[side, 40:41, :] = value[NX + 1 : NX + 2]
        here = value[:NX]
        lower, upper = halo[side, 7:39, :], halo[side, 9:41, :]
        kick = table[2] * (here - lower) + table[3] * (here - upper)
        kicks[side] = -explicit_part * (kick + lane_stencil(here, thick))
    if last:
        temp_buffer, cure_buffer, sems = rest[5:8]
    copies = []
    for block in range(4):
        span = slice(block * 16, block * 16 + 16)
        left, right = spikes[0, span, :], spikes[1, span, :]

        def step(i, carry):
            delta = left * halo[0, pl.ds(i + 8, 1), :] + right * halo[1, pl.ds(i + 8, 1), :]
            kick = left * kicks[0, pl.ds(i, 1), :] + right * kicks[1, pl.ds(i, 1), :]
            value = base[i, span, :] + (gain[i, span, :] + explicit_part) * delta + kick
            cure_value = cure_base[i, span, :] + cure_gain[i, span, :] * delta
            if last:
                temp_buffer[block, i] = value
                cure_buffer[block, i] = cure_value
                return carry
            temp_out[i, span, :] = value
            cure_out[i, span, :] = cure_value
            low, high = carry
            return low + inv[i, 0] * value, high + inv[i, NX - 1] * value

        zero = jnp.zeros((16, NZ), jnp.float32)
        carry = lax.fori_loop(0, NX, step, () if last else (zero, zero), unroll=4)
        if last:
            for buffer, out, sem in (
                (temp_buffer, temp_out, sems.at[block, 0]),
                (cure_buffer, cure_out, sems.at[block, 1]),
            ):
                copy = pltpu.make_async_copy(buffer.at[block], out.at[:, span, :], sem)
                copy.start()
                copies.append(copy)
        else:
            refs[14][0, span, :] = carry[0]
            refs[14][1, span, :] = carry[1]
    for copy in copies:
        copy.wait()
    if not last:
        x_end_rows(refs[14], inv, faces)


def ring_of(axis, count, index):
    size = lax.axis_size(axis)
    pairs = []
    for shift in range(1, count):
        move = []
        for device in range(size):
            rest, at = index(device)
            targets = [d for d in range(size) if index(d) == (rest, (at + shift) % count)]
            move.append((device, targets[0]))
        pairs.append(move)
    return pairs


def exchange(message, axis, count, index):
    return [message] + [lax.ppermute(message, axis, move) for move in ring_of(axis, count, index)]


def along_z(device):
    return device // 4, device % 4


def along_y(device):
    return device % 4, device // 4


def along_core(device):
    return device // 2, device % 2


def along_x(device):
    return device % 2, device // 2


def per_device(
    temper_start,
    cure_start,
    temper_middle,
    cure_middle,
    adjoint_temper,
    adjoint_cure,
    conduct_first,
    inverse_first,
    conduct_second,
    inverse_second,
    conduct_thick,
    inverse_thick,
):
    gx, gy = lax.axis_index("gx"), lax.axis_index("gy")
    place_z, place_y = (gx % 4).reshape(1), (gx // 4).reshape(1)
    place_core, place_x = (gy % 2).reshape(1), (gy // 2).reshape(1)
    tips = call(
        tips_kernel,
        "tips",
        (inverse_first, conduct_first, adjoint_temper),
        (smem, smem, vmem),
        [f32(2, ROWS_X, NZ)],
    )[0]
    temp, cure_adj = adjoint_temper, adjoint_cure
    table, spikes, thick_high, thick_low, second_matrix, thick = call(
        prepare_kernel,
        "prepare",
        (
            inverse_first,
            conduct_first,
            inverse_second,
            conduct_second,
            inverse_thick,
            inverse_second.T,
            conduct_thick.reshape(1, NZ + 1),
        ),
        (*[smem] * 4, *[vmem] * 3),
        [
            f32(6, NX, NZ),
            f32(2, NY, NZ),
            bf16(NZ, NZ),
            bf16(NZ, NZ),
            bf16(NY, 3 * NY),
            f32(8, NZ),
        ],
    )
    fields = ((temper_middle, cure_middle), (temper_start, cure_start))
    for number, (temper, cure) in enumerate(fields):
        last = number == 1
        ring = exchange(tips, "gx", 4, along_z)
        (through,) = call(
            solve_z_kernel,
            "solve_z",
            (temp, thick_high, thick_low),
            [vmem] * 3,
            [f32(NX, NY, NZ)],
            flops=int(1.6e9),
        )
        gain, cure_gain = call(
            rates_kernel, "rates", (temper, cure), [vmem] * 2, [f32(NX, NY, NZ)] * 2, flops=int(1e9)
        )
        tips, own = call(
            functools.partial(chain_kernel, 4, DATA_X),
            "chain_z",
            (place_z, *ring),
            (smem, *[vmem] * 4),
            [f32(2, ROWS_X, NZ)] * 2,
            chain_scratch(4, ROWS_X),
        )
        ring = exchange(tips, "gx", 4, along_y)
        second_done, second_tips = call(
            solve_y_kernel,
            "solve_y",
            (through, second_matrix, inverse_first),
            [vmem] * 3,
            [f32(NX, NY, NZ), f32(2, NX, NZ)],
            [pltpu.VMEM((2, NX, NZ), jnp.float32)],
            flops=int(1.6e9),
        )
        message, halo_through, halo_second = call(
            middle_kernel,
            "middle",
            (place_y, inverse_second, conduct_second, *ring, own, thick_high, thick_low, second_matrix, second_tips, table),
            (smem, smem, smem, *[vmem] * 10),
            [f32(2, ROWS_Y, NZ), f32(2, NY, NZ), f32(2, NY, NZ)],
            chain_scratch(4, ROWS_X) + [pltpu.VMEM((2, NY, NZ), jnp.float32)],
        )
        pair = exchange(message, "gy", 2, along_core)
        message, own = call(
            functools.partial(chain_kernel, 2, DATA_Y),
            "chain_core",
            (place_core, *pair),
            (smem, *[vmem] * 2),
            [f32(2, ROWS_Y, NZ)] * 2,
            chain_scratch(2, ROWS_Y),
        )
        ring = exchange(message, "gy", 4, along_x)
        base, cure_base = call(
            local_kernel,
            "local",
            (conduct_first, second_done, through, temp, cure_adj, gain, cure_gain, halo_second, halo_through, table, thick),
            (smem, *[vmem] * 10),
            [f32(NX, NY, NZ)] * 2,
            [pltpu.VMEM((NX, 16, NZ), jnp.float32)] * 2,
            flops=int(1.6e9),
            limit=20,
        )
        outs = [f32(NX, NY, NZ)] * 2 + ([] if last else [f32(2, ROWS_X, NZ)])
        buffers = [pltpu.VMEM((4, NX, 16, NZ), jnp.float32)] * 2 + [pltpu.SemaphoreType.DMA((4, 2))]
        results = call(
            functools.partial(final_kernel, last),
            "final",
            (place_x, inverse_first, conduct_first, *ring, own, base, gain, cure_base, cure_gain, spikes, table, thick),
            (smem, smem, smem, *[vmem] * 12),
            outs,
            chain_scratch(4, ROWS_Y)
            + [pltpu.VMEM((2, 48, NZ), jnp.float32), pltpu.VMEM((2, NX, NZ), jnp.float32)]
            + (buffers if last else []),
            limit=20,
            out_space=pl.BlockSpec(memory_space=pl.ANY) if last else vmem,
        )
        temp, cure_adj = results[0], results[1]
        if not last:
            tips = results[2]
    return (temp, cure_adj)


def solution(mesh):
    placed = (
        P("gx", "gy", None),
        P("gx", "gy", None),
        P("gx", "gy", None),
        P("gx", "gy", None),
        P("gx", "gy", None),
        P("gx", "gy", None),
        P("gx"),
        P("gx", None),
        P("gy"),
        P("gy", None),
        P(),
        P(),
    )
    return jax.shard_map(
        per_device,
        mesh=mesh,
        in_specs=placed,
        out_specs=(P("gx", "gy", None), P("gx", "gy", None)),
        check_vma=False,
    )
```

```python
import functools

import jax
import jax.numpy as jnp
from jax import lax
from jax.experimental import pallas as pl
from jax.experimental.pallas import tpu as pltpu
from jax.sharding import PartitionSpec as P

explicit_part = 2.0
heat_release = 100.0
cure_step = 0.5
arrhenius = 0.5
initial_rate = 0.1
highest = lax.Precision.HIGHEST

NX, NY, NZ = 32, 64, 256
ROWS_X, ROWS_Y = 72, 40
DATA_X, DATA_Y = 64, 34
MIB = 1024 * 1024


vmem = pl.BlockSpec(memory_space=pltpu.VMEM)
smem = pl.BlockSpec(memory_space=pltpu.SMEM)


def f32(*shape):
    return jax.ShapeDtypeStruct(shape, jnp.float32)


def bf16(*shape):
    return jax.ShapeDtypeStruct(shape, jnp.bfloat16)


def call(kernel, name, operands, in_specs, outs, scratch=(), flops=0, limit=12 * MIB, out_space=vmem):
    size = sum(x.size * 4 for x in operands) + sum(o.size * 4 for o in outs)
    return pl.pallas_call(
        kernel,
        name=name,
        out_shape=tuple(outs),
        in_specs=list(in_specs),
        out_specs=tuple([out_space] * len(outs)),
        scratch_shapes=list(scratch),
        compiler_params=pltpu.CompilerParams(vmem_limit_bytes=limit),
        cost_estimate=pl.CostEstimate(flops=flops, bytes_accessed=size, transcendentals=0),
    )(*operands)


def place_on(axis, low, mask):
    return lax.bitwise_and(lax.shift_right_logical(lax.axis_index(axis), low), mask)


def chain(count, place, parts, data, gather, alphas, betas):
    rows = gather.shape[2]
    masks = (0, 1) if count == 2 else (0, *(1, 3, 2))
    for mask, part in zip(masks, parts):
        gather[lax.bitwise_xor(place, mask)] = part[...]
    row = lax.broadcasted_iota(jnp.int32, (rows, NZ), 0)
    is_left, is_right = row == data, row == data + 1

    def source(j, end):
        value = gather[j, end]
        if j != 0:
            value = jnp.where(is_left, 0.0, value)
        if j != count - 1:
            value = jnp.where(is_right, 0.0, value)
        return value

    def coefficient(j, end, side):
        return gather[j, end, data + side : data + side + 1, :]

    first = [source(j, 0) for j in range(count)]
    last = [source(j, 1) for j in range(count)]
    left_first = [coefficient(j, 0, 0) for j in range(count)]
    left_last = [coefficient(j, 1, 0) for j in range(count)]
    right_first = [coefficient(j, 0, 1) for j in range(count)]
    right_last = [coefficient(j, 1, 1) for j in range(count)]

    pre, corner = [last[0]], [right_last[0]]
    for t in range(1, count):
        inv = 1.0 / (1.0 - corner[-1] * left_first[t])
        gain = left_last[t] * inv
        pre.append(last[t] + gain * (pre[-1] + corner[-1] * first[t]))
        corner.append(right_last[t] + gain * corner[-1] * right_first[t])
    post, bend = {count - 1: first[-1]}, {count - 1: left_first[-1]}
    for t in range(count - 2, -1, -1):
        e, g = post[t + 1], bend[t + 1]
        gain = right_first[t] / (1.0 - g * right_last[t])
        post[t] = first[t] + gain * (e + g * last[t])
        bend[t] = left_first[t] + gain * g * left_last[t]
    alphas[0] = jnp.where(is_left, 1.0, jnp.zeros((rows, NZ), jnp.float32))
    betas[count - 1] = jnp.where(is_right, 1.0, jnp.zeros((rows, NZ), jnp.float32))
    for t in range(count - 1):
        a, c, e, g = pre[t], corner[t], post[t + 1], bend[t + 1]
        inv = 1.0 / (1.0 - c * g)
        alphas[t + 1] = (a + c * e) * inv
        betas[t] = (e + g * a) * inv
    return post[0], pre[-1], alphas[place], betas[place]


def chain_scratch(count, rows):
    return [
        pltpu.VMEM((count, 2, rows, NZ), jnp.float32),
        pltpu.VMEM((count, rows, NZ), jnp.float32),
        pltpu.VMEM((count, rows, NZ), jnp.float32),
    ]


def end_rows(out, end, start, left, right):
    row = lax.broadcasted_iota(jnp.int32, (8, NZ), 0)
    block = jnp.where(row == 0, left, jnp.where(row == 1, right, 0.0))
    out[end, start : start + 8, :] = block


def tips_kernel(field_hbm, inv_hbm, faces_hbm, out, inv, faces, field, sems):
    small = [
        pltpu.make_async_copy(inv_hbm, inv, sems.at[4]),
        pltpu.make_async_copy(faces_hbm, faces, sems.at[5]),
    ]
    large = []
    for block in range(4):
        span = slice(block * 16, block * 16 + 16)
        large.append(
            pltpu.make_async_copy(field_hbm.at[:, span, :], field.at[:, span, :], sems.at[block])
        )
    for copy in small + large:
        copy.start()
    for copy in small:
        copy.wait()
    for block in range(4):
        span = slice(block * 16, block * 16 + 16)
        large[block].wait()
        low = inv[0, 0] * field[0, span, :]
        high = inv[0, NX - 1] * field[0, span, :]
        for i in range(1, NX):
            value = field[i, span, :]
            low = low + inv[i, 0] * value
            high = high + inv[i, NX - 1] * value
        out[0, span, :] = low
        out[1, span, :] = high
    end_rows(out, 0, DATA_X, faces[0] * inv[0, 0], faces[NX] * inv[NX - 1, 0])
    end_rows(out, 1, DATA_X, faces[0] * inv[0, NX - 1], faces[NX] * inv[NX - 1, NX - 1])


def chain_kernel(count, data, place, *refs):
    parts, (tips, own), scratch = refs[:count], refs[count : count + 2], refs[count + 2 :]
    e, a, alpha, beta = chain(count, place_on(*place), parts, data, *scratch)
    tips[0] = e
    tips[1] = a
    own[0] = alpha
    own[1] = beta


def split(value):
    high = value.astype(jnp.bfloat16)
    return high, (value - high.astype(jnp.float32)).astype(jnp.bfloat16)


def product(left, right):
    return jnp.dot(left, right, preferred_element_type=jnp.float32)


def times_thick(value, thick_high, thick_low):
    high, low = split(value)
    total = product(low, thick_high[...]) + product(high, thick_low[...])
    return total + product(high, thick_high[...])


def times_second(second, value):
    high, low = split(value)
    return product(second[...], jnp.concatenate([high, high, low], axis=0))


def prepare_kernel(
    inv, faces, inv_second, faces_second, inverse_thick, inverse_t, thick,
    table, spikes, thick_high, thick_low, second, thick_rows,
):
    def row(value):
        return jnp.full((1, NZ), value, jnp.float32)

    delta = row(1.0 + faces[0] + faces[1])
    for i in range(NX):
        table[0, i : i + 1, :] = row(faces[0] * inv[0, i])
        table[1, i : i + 1, :] = row(faces[NX] * inv[NX - 1, i])
        table[2, i : i + 1, :] = row(faces[i])
        table[3, i : i + 1, :] = row(faces[i + 1])
        table[6, i : i + 1, :] = row(inv[i, 0])
        table[7, i : i + 1, :] = row(inv[i, NX - 1])
        inverse = 1.0 / delta
        table[5, i : i + 1, :] = inverse
        ratio = faces[i + 1] * inverse
        table[4, i : i + 1, :] = ratio
        if i < NX - 1:
            delta = 1.0 + faces[i + 1] + faces[i + 2] - faces[i + 1] * ratio
    for y in range(NY):
        spikes[0, y : y + 1, :] = row(faces_second[0] * inv_second[0, y])
        spikes[1, y : y + 1, :] = row(faces_second[NY] * inv_second[NY - 1, y])
    thick_high[...], thick_low[...] = split(inverse_thick[...])
    high, low = split(inverse_t[...].T)
    second[...] = jnp.concatenate([high, low, high], axis=1)
    below = thick[0:NZ].reshape(1, NZ)
    above = thick[1 : NZ + 1].reshape(1, NZ)
    lane = lax.broadcasted_iota(jnp.int32, (1, NZ), 1)
    thick_rows[0:1, :] = below
    thick_rows[1:2, :] = above
    thick_rows[2:3, :] = below + above
    thick_rows[3:4, :] = jnp.where(lane == 0, 0.0, below)
    thick_rows[4:5, :] = jnp.where(lane == NZ - 1, 0.0, above)


def rates_kernel(temper, cure, gain, cure_gain):
    @pl.loop(0, NX, unroll=2)
    def _(i):
        c = cure[i]
        heating = jnp.exp(arrhenius * temper[i])
        remain = 1.0 - c
        heated = heating * remain
        ready = initial_rate + c
        gain[i] = (heat_release * arrhenius) * (heated * ready * remain)
        cure_gain[i] = heat_release * (heated * (remain - 2.0 * ready))


def solve_z_kernel(field, thick_high, thick_low, out):
    @pl.loop(0, 8)
    def _(block):
        span = pl.ds(block * 4, 4)
        value = field[span].reshape(4 * NY, NZ)
        out[span] = times_thick(value, thick_high, thick_low).reshape(4, NY, NZ)


def solve_y_kernel(field, second, out):
    @pl.loop(0, NX, unroll=4)
    def _(i):
        out[i] = times_second(second, field[i])


def solve_x_kernel(second_done, through, table, solved, residual, tips, work, work_through):
    zero = jnp.zeros((16, NZ), jnp.float32)
    for block in range(4):
        span = slice(block * 16, block * 16 + 16)

        def forward(i, carry):
            value, whole, ratio = carry
            value = second_done[i, span, :] + ratio * value
            whole = through[i, span, :] + ratio * whole
            work[i] = value
            work_through[i] = whole
            return value, whole, table[4, pl.ds(i, 1), :]

        lax.fori_loop(0, NX, forward, (zero, zero, jnp.zeros((1, NZ), jnp.float32)), unroll=4)

        def backward(step, carry):
            i = NX - 1 - step
            value, whole = carry
            inverse, ratio = table[5, pl.ds(i, 1), :], table[4, pl.ds(i, 1), :]
            value = inverse * work[i] + ratio * value
            whole = inverse * work_through[i] + ratio * whole
            solved[i, span, :] = value
            residual[i, span, :] = (second_done[i, span, :] - value) + (whole - value)
            if block == 0:
                tips[0, pl.ds(i, 1), :] = value[0:1]
            if block == 3:
                tips[1, pl.ds(i, 1), :] = value[15:16]
            return value, whole

        lax.fori_loop(0, NX, backward, (zero, zero), unroll=4)


def middle_kernel(*refs):
    parts = refs[:4]
    own, thick_high, thick_low, second_matrix, tips, table, spikes = refs[4:11]
    out, through, second = refs[11:14]
    scratch = refs[14:17]
    halo = refs[17]
    unused, unused, p, n = chain(4, place_on("gx", 2, 3), parts, DATA_X, *scratch)
    p, n = p[:DATA_X], n[:DATA_X]
    for side in range(2):
        halo[side] = (
            own[side, :DATA_X, :]
            + own[side, DATA_X : DATA_X + 1, :] * p
            + own[side, DATA_X + 1 : DATA_X + 2, :] * n
        )
    through[...] = times_thick(
        halo[...].reshape(2 * NY, NZ), thick_high, thick_low
    ).reshape(2, NY, NZ)
    for side in range(2):
        second[side] = times_second(second_matrix, through[side])
    for end in range(2):
        y = end * (NY - 1)
        prev_row, next_row = second[0, y : y + 1, :], second[1, y : y + 1, :]
        out[end, :NX, :] = tips[end] + table[0] * prev_row + table[1] * next_row
        row = lax.broadcasted_iota(jnp.int32, (8, NZ), 0)
        left, right = spikes[0, y : y + 1, :], spikes[1, y : y + 1, :]
        out[end, NX:, :] = jnp.where(
            row == 0,
            prev_row,
            jnp.where(row == 1, next_row, jnp.where(row == 2, left, jnp.where(row == 3, right, 0.0))),
        )


def lane_stencil(value, thick):
    lower, upper = pltpu.roll(value, 1, 1), pltpu.roll(value, NZ - 1, 1)
    return thick[2:3, :] * value - thick[3:4, :] * lower - thick[4:5, :] * upper


def local_kernel(
    solved, residual, temp, cure_adj, gain, cure_gain, second, halo_through, table, thick,
    base, cure_base,
):
    for block in range(4):
        span = slice(block * 16, block * 16 + 16)
        prev_value, next_value = second[0, span, :], second[1, span, :]
        prev_rest = halo_through[0, span, :] - 2.0 * prev_value
        next_rest = halo_through[1, span, :] - 2.0 * next_value

        @pl.loop(0, NX, unroll=4)
        def _(i):
            left, right = table[0, pl.ds(i, 1), :], table[1, pl.ds(i, 1), :]
            value = solved[i, span, :] + left * prev_value + right * next_value
            kick = residual[i, span, :] + left * prev_rest + right * next_rest
            kick = kick + lane_stencil(value, thick)
            lc = cure_adj[i, span, :]
            source = value + (cure_step / heat_release) * lc
            base[i, span, :] = temp[i, span, :] - explicit_part * kick + gain[i, span, :] * source
            cure_base[i, span, :] = lc + cure_gain[i, span, :] * source


def final_kernel(last, *refs):
    parts = refs[:4]
    own, base, gain, cure_base, cure_gain, spikes, table, thick = refs[4:12]
    outs = 2 if last else 3
    temp_out, cure_out = refs[12:14]
    rest = refs[12 + outs :]
    scratch, halo, kicks = rest[:3], rest[3], rest[4]
    unused, unused, p, n = chain(4, place_on("gy", 1, 3), parts, DATA_Y, *scratch)
    for side in range(2):
        value = (
            own[side]
            + own[side, DATA_Y : DATA_Y + 1, :] * p
            + own[side, DATA_Y + 1 : DATA_Y + 2, :] * n
        )
        halo[side, 8:40, :] = value[:NX]
        halo[side, 7:8, :] = value[NX : NX + 1]
        halo[side, 40:41, :] = value[NX + 1 : NX + 2]
        here = value[:NX]
        lower, upper = halo[side, 7:39, :], halo[side, 9:41, :]
        kick = table[2] * (here - lower) + table[3] * (here - upper)
        kicks[side] = -explicit_part * (kick + lane_stencil(here, thick))
    if last:
        temp_buffer, cure_buffer, sems = rest[5:8]
    copies = []
    for block in range(4):
        span = slice(block * 16, block * 16 + 16)
        left, right = spikes[0, span, :], spikes[1, span, :]

        def step(i, carry):
            delta = left * halo[0, pl.ds(i + 8, 1), :] + right * halo[1, pl.ds(i + 8, 1), :]
            kick = left * kicks[0, pl.ds(i, 1), :] + right * kicks[1, pl.ds(i, 1), :]
            value = base[i, span, :] + (gain[i, span, :] + explicit_part) * delta + kick
            cure_value = cure_base[i, span, :] + cure_gain[i, span, :] * delta
            if last:
                temp_buffer[block, i] = value
                cure_buffer[block, i] = cure_value
                return carry
            temp_out[i, span, :] = value
            cure_out[i, span, :] = cure_value
            low, high = carry
            low = low + table[6, pl.ds(i, 1), :] * value
            return low, high + table[7, pl.ds(i, 1), :] * value

        zero = jnp.zeros((16, NZ), jnp.float32)
        carry = lax.fori_loop(0, NX, step, () if last else (zero, zero), unroll=4)
        if last:
            for buffer, out, sem in (
                (temp_buffer, temp_out, sems.at[block, 0]),
                (cure_buffer, cure_out, sems.at[block, 1]),
            ):
                copy = pltpu.make_async_copy(buffer.at[block], out.at[:, span, :], sem)
                copy.start()
                copies.append(copy)
        else:
            refs[14][0, span, :] = carry[0]
            refs[14][1, span, :] = carry[1]
    for copy in copies:
        copy.wait()
    if not last:
        for end, i in ((0, 0), (1, NX - 1)):
            end_rows(
                refs[14], end, DATA_X, table[0, i : i + 1, :], table[1, i : i + 1, :]
            )


def exchange(message, axis, count, index):
    size = lax.axis_size(axis)
    at = {index(device): device for device in range(size)}
    received = [message]
    for mask in (1,) if count == 2 else (1, 3, 2):
        move = [(at[(rest, here)], at[(rest, here ^ mask)]) for rest, here in at]
        received.append(lax.ppermute(message, axis, move))
    return received


def along_z(device):
    return device // 4, device % 4


def along_y(device):
    return device % 4, device // 4


def along_core(device):
    return device // 2, device % 2


def along_x(device):
    return device % 2, device // 2


def per_device(
    temper_start,
    cure_start,
    temper_middle,
    cure_middle,
    adjoint_temper,
    adjoint_cure,
    conduct_first,
    inverse_first,
    conduct_second,
    inverse_second,
    conduct_thick,
    inverse_thick,
):
    hbm = pl.BlockSpec(memory_space=pltpu.HBM)
    (tips,) = call(
        tips_kernel,
        "tips",
        (adjoint_temper, inverse_first, conduct_first),
        (hbm, hbm, hbm),
        [f32(2, ROWS_X, NZ)],
        [
            pltpu.SMEM((NX, NX), jnp.float32),
            pltpu.SMEM((NX + 1,), jnp.float32),
            pltpu.VMEM((NX, NY, NZ), jnp.float32),
            pltpu.SemaphoreType.DMA((6,)),
        ],
        limit=65400000,
    )
    temp, cure_adj = adjoint_temper, adjoint_cure
    table, spikes, thick_high, thick_low, second_matrix, thick = call(
        prepare_kernel,
        "prepare",
        (
            inverse_first,
            conduct_first,
            inverse_second,
            conduct_second,
            inverse_thick,
            inverse_second,
            conduct_thick,
        ),
        (*[smem] * 4, *[vmem] * 3),
        [
            f32(8, NX, NZ),
            f32(2, NY, NZ),
            bf16(NZ, NZ),
            bf16(NZ, NZ),
            bf16(NY, 3 * NY),
            f32(8, NZ),
        ],
    )
    fields = ((temper_middle, cure_middle), (temper_start, cure_start))
    for number, (temper, cure) in enumerate(fields):
        last = number == 1
        ring = exchange(tips, "gx", 4, along_z)
        (through,) = call(
            solve_z_kernel,
            "solve_z",
            (temp, thick_high, thick_low),
            [vmem] * 3,
            [f32(NX, NY, NZ)],
            flops=int(1.6e9),
        )
        gain, cure_gain = call(
            rates_kernel, "rates", (temper, cure), [vmem] * 2, [f32(NX, NY, NZ)] * 2, flops=int(1e9)
        )
        tips, own = call(
            functools.partial(chain_kernel, 4, DATA_X, ("gx", 0, 3)),
            "chain_z",
            ring,
            [vmem] * 4,
            [f32(2, ROWS_X, NZ)] * 2,
            chain_scratch(4, ROWS_X),
        )
        ring = exchange(tips, "gx", 4, along_y)
        (second_done,) = call(
            solve_y_kernel,
            "solve_y",
            (through, second_matrix),
            [vmem] * 2,
            [f32(NX, NY, NZ)],
            flops=int(1.6e9),
        )
        solved, residual, second_tips = call(
            solve_x_kernel,
            "solve_x",
            (second_done, through, table),
            [vmem] * 3,
            [f32(NX, NY, NZ), f32(NX, NY, NZ), f32(2, NX, NZ)],
            [pltpu.VMEM((NX, 16, NZ), jnp.float32)] * 2,
            flops=int(1e9),
        )
        message, halo_through, halo_second = call(
            middle_kernel,
            "middle",
            (*ring, own, thick_high, thick_low, second_matrix, second_tips, table, spikes),
            [vmem] * 11,
            [f32(2, ROWS_Y, NZ), f32(2, NY, NZ), f32(2, NY, NZ)],
            chain_scratch(4, ROWS_X) + [pltpu.VMEM((2, NY, NZ), jnp.float32)],
        )
        pair = exchange(message, "gy", 2, along_core)
        message, own = call(
            functools.partial(chain_kernel, 2, DATA_Y, ("gy", 0, 1)),
            "chain_core",
            pair,
            [vmem] * 2,
            [f32(2, ROWS_Y, NZ)] * 2,
            chain_scratch(2, ROWS_Y),
        )
        ring = exchange(message, "gy", 4, along_x)
        base, cure_base = call(
            local_kernel,
            "local",
            (solved, residual, temp, cure_adj, gain, cure_gain, halo_second, halo_through, table, thick),
            [vmem] * 10,
            [f32(NX, NY, NZ)] * 2,
            flops=int(1.6e9),
            limit=20 * MIB,
        )
        outs = [f32(NX, NY, NZ)] * 2 + ([] if last else [f32(2, ROWS_X, NZ)])
        buffers = [pltpu.VMEM((4, NX, 16, NZ), jnp.float32)] * 2 + [pltpu.SemaphoreType.DMA((4, 2))]
        results = call(
            functools.partial(final_kernel, last),
            "final",
            (*ring, own, base, gain, cure_base, cure_gain, spikes, table, thick),
            [vmem] * 12,
            outs,
            chain_scratch(4, ROWS_Y)
            + [pltpu.VMEM((2, 48, NZ), jnp.float32), pltpu.VMEM((2, NX, NZ), jnp.float32)]
            + (buffers if last else []),
            limit=20 * MIB,
            out_space=pl.BlockSpec(memory_space=pl.ANY) if last else vmem,
        )
        temp, cure_adj = results[0], results[1]
        if not last:
            tips = results[2]
    return (temp, cure_adj)


def solution(mesh):
    placed = (
        P("gx", "gy", None),
        P("gx", "gy", None),
        P("gx", "gy", None),
        P("gx", "gy", None),
        P("gx", "gy", None),
        P("gx", "gy", None),
        P("gx"),
        P("gx", None),
        P("gy"),
        P("gy", None),
        P(),
        P(),
    )
    return jax.shard_map(
        per_device,
        mesh=mesh,
        in_specs=placed,
        out_specs=(P("gx", "gy", None), P("gx", "gy", None)),
        check_vma=False,
    )
```

```python
import functools

import jax
import jax.numpy as jnp
from jax import lax
from jax.experimental import pallas as pl
from jax.experimental.pallas import tpu as pltpu
from jax.sharding import PartitionSpec as P

explicit_part = 2.0
heat_release = 100.0
cure_step = 0.5
arrhenius = 0.5
initial_rate = 0.1
highest = lax.Precision.HIGHEST

NX, NY, NZ = 32, 64, 256
ROWS_X, ROWS_Y = 72, 40
DATA_X, DATA_Y = 64, 34
MIB = 1024 * 1024


vmem = pl.BlockSpec(memory_space=pltpu.VMEM)
smem = pl.BlockSpec(memory_space=pltpu.SMEM)
anywhere = pl.BlockSpec(memory_space=pl.ANY)


def f32(*shape):
    return jax.ShapeDtypeStruct(shape, jnp.float32)


def bf16(*shape):
    return jax.ShapeDtypeStruct(shape, jnp.bfloat16)


def call(kernel, name, operands, in_specs, outs, scratch=(), flops=0, limit=12 * MIB, out_space=vmem):
    size = sum(x.size * 4 for x in operands) + sum(o.size * 4 for o in outs)
    return pl.pallas_call(
        kernel,
        name=name,
        out_shape=tuple(outs),
        in_specs=list(in_specs),
        out_specs=tuple([out_space] * len(outs)),
        scratch_shapes=list(scratch),
        compiler_params=pltpu.CompilerParams(vmem_limit_bytes=limit),
        cost_estimate=pl.CostEstimate(flops=flops, bytes_accessed=size, transcendentals=0),
    )(*operands)


def place_on(axis, low, mask):
    return lax.bitwise_and(lax.shift_right_logical(lax.axis_index(axis), low), mask)


def chain(count, place, parts, data, gather, alphas, betas):
    rows = gather.shape[2]
    masks = (0, 1) if count == 2 else (0, *(2, 3, 1))
    for mask, part in zip(masks, parts):
        gather[lax.bitwise_xor(place, mask)] = part[...]
    row = lax.broadcasted_iota(jnp.int32, (rows, NZ), 0)
    is_left, is_right = row == data, row == data + 1

    def source(j, end):
        value = gather[j, end]
        if j != 0:
            value = jnp.where(is_left, 0.0, value)
        if j != count - 1:
            value = jnp.where(is_right, 0.0, value)
        return value

    def coefficient(j, end, side):
        return gather[j, end, data + side : data + side + 1, :]

    first = [source(j, 0) for j in range(count)]
    last = [source(j, 1) for j in range(count)]
    left_first = [coefficient(j, 0, 0) for j in range(count)]
    left_last = [coefficient(j, 1, 0) for j in range(count)]
    right_first = [coefficient(j, 0, 1) for j in range(count)]
    right_last = [coefficient(j, 1, 1) for j in range(count)]

    pre, corner = [last[0]], [right_last[0]]
    for t in range(1, count):
        inv = 1.0 / (1.0 - corner[-1] * left_first[t])
        gain = left_last[t] * inv
        pre.append(last[t] + gain * (pre[-1] + corner[-1] * first[t]))
        corner.append(right_last[t] + gain * corner[-1] * right_first[t])
    post, bend = {count - 1: first[-1]}, {count - 1: left_first[-1]}
    for t in range(count - 2, -1, -1):
        e, g = post[t + 1], bend[t + 1]
        gain = right_first[t] / (1.0 - g * right_last[t])
        post[t] = first[t] + gain * (e + g * last[t])
        bend[t] = left_first[t] + gain * g * left_last[t]
    alphas[0] = jnp.where(is_left, 1.0, jnp.zeros((rows, NZ), jnp.float32))
    betas[count - 1] = jnp.where(is_right, 1.0, jnp.zeros((rows, NZ), jnp.float32))
    for t in range(count - 1):
        a, c, e, g = pre[t], corner[t], post[t + 1], bend[t + 1]
        inv = 1.0 / (1.0 - c * g)
        alphas[t + 1] = (a + c * e) * inv
        betas[t] = (e + g * a) * inv
    return post[0], pre[-1], alphas[place], betas[place]


def chain_scratch(count, rows):
    return [
        pltpu.VMEM((count, 2, rows, NZ), jnp.float32),
        pltpu.VMEM((count, rows, NZ), jnp.float32),
        pltpu.VMEM((count, rows, NZ), jnp.float32),
    ]


def end_rows(out, end, start, left, right):
    row = lax.broadcasted_iota(jnp.int32, (8, NZ), 0)
    block = jnp.where(row == 0, left, jnp.where(row == 1, right, 0.0))
    out[end, start : start + 8, :] = block


def tips_kernel(field_hbm, inv_hbm, faces_hbm, out, inv, faces, field, sems):
    small = [
        pltpu.make_async_copy(inv_hbm, inv, sems.at[4]),
        pltpu.make_async_copy(faces_hbm, faces, sems.at[5]),
    ]
    large = []
    for block in range(4):
        span = slice(block * 16, block * 16 + 16)
        large.append(
            pltpu.make_async_copy(field_hbm.at[:, span, :], field.at[:, span, :], sems.at[block])
        )
    for copy in small + large:
        copy.start()
    for copy in small:
        copy.wait()
    for block in range(4):
        span = slice(block * 16, block * 16 + 16)
        large[block].wait()
        low = inv[0, 0] * field[0, span, :]
        high = inv[0, NX - 1] * field[0, span, :]
        for i in range(1, NX):
            value = field[i, span, :]
            low = low + inv[i, 0] * value
            high = high + inv[i, NX - 1] * value
        out[0, span, :] = low
        out[1, span, :] = high
    end_rows(out, 0, DATA_X, faces[0] * inv[0, 0], faces[NX] * inv[NX - 1, 0])
    end_rows(out, 1, DATA_X, faces[0] * inv[0, NX - 1], faces[NX] * inv[NX - 1, NX - 1])


def chain_kernel(count, data, place, *refs):
    parts, (tips, own), scratch = refs[:count], refs[-5:-3], refs[-3:]
    e, a, alpha, beta = chain(count, place_on(*place), parts, data, *scratch)
    tips[0] = e
    tips[1] = a
    own[0] = alpha
    own[1] = beta


def split(value):
    high = value.astype(jnp.bfloat16)
    return high, (value - high.astype(jnp.float32)).astype(jnp.bfloat16)


def product(left, right):
    return jnp.dot(left, right, preferred_element_type=jnp.float32)


def times_thick(value, thick_high, thick_low):
    high, low = split(value)
    total = product(low, thick_high[...]) + product(high, thick_low[...])
    return total + product(high, thick_high[...])


def times_second(second, value):
    high, low = split(value)
    return product(second[...], jnp.concatenate([high, high, low], axis=0))


def prepare_thick_kernel(inverse_thick, thick_high, thick_low):
    thick_high[...], thick_low[...] = split(inverse_thick[...])


def prepare_kernel(
    inv, faces, inv_second, faces_second, inverse_t, thick, unused,
    table, spikes, second, thick_rows,
):
    def row(value):
        return jnp.full((1, NZ), value, jnp.float32)

    delta = row(1.0 + faces[0] + faces[1])
    for i in range(NX):
        table[0, i : i + 1, :] = row(faces[0] * inv[0, i])
        table[1, i : i + 1, :] = row(faces[NX] * inv[NX - 1, i])
        table[2, i : i + 1, :] = row(faces[i])
        table[3, i : i + 1, :] = row(faces[i + 1])
        table[6, i : i + 1, :] = row(inv[i, 0])
        table[7, i : i + 1, :] = row(inv[i, NX - 1])
        inverse = 1.0 / delta
        table[5, i : i + 1, :] = inverse
        ratio = faces[i + 1] * inverse
        table[4, i : i + 1, :] = ratio
        if i < NX - 1:
            delta = 1.0 + faces[i + 1] + faces[i + 2] - faces[i + 1] * ratio
    for y in range(NY):
        spikes[0, y : y + 1, :] = row(faces_second[0] * inv_second[0, y])
        spikes[1, y : y + 1, :] = row(faces_second[NY] * inv_second[NY - 1, y])
    high, low = split(inverse_t[...].T)
    second[...] = jnp.concatenate([high, low, high], axis=1)
    below = thick[0:NZ].reshape(1, NZ)
    above = thick[1 : NZ + 1].reshape(1, NZ)
    lane = lax.broadcasted_iota(jnp.int32, (1, NZ), 1)
    thick_rows[0:1, :] = below
    thick_rows[1:2, :] = above
    thick_rows[2:3, :] = below + above
    thick_rows[3:4, :] = jnp.where(lane == 0, 0.0, below)
    thick_rows[4:5, :] = jnp.where(lane == NZ - 1, 0.0, above)


def rates_kernel(temper, cure, unused, gain, cure_gain):
    @pl.loop(0, NX, unroll=2)
    def _(i):
        c = cure[i]
        heating = jnp.exp(arrhenius * temper[i])
        remain = 1.0 - c
        heated = heating * remain
        ready = initial_rate + c
        gain[i] = (heat_release * arrhenius) * (heated * ready * remain)
        cure_gain[i] = heat_release * (heated * (remain - 2.0 * ready))


def solve_z_kernel(field, thick_high, thick_low, out):
    @pl.loop(0, 8)
    def _(block):
        span = pl.ds(block * 4, 4)
        value = field[span].reshape(4 * NY, NZ)
        out[span] = times_thick(value, thick_high, thick_low).reshape(4, NY, NZ)


def solve_y_kernel(field, second, out):
    @pl.loop(0, NX, unroll=4)
    def _(i):
        out[i] = times_second(second, field[i])


def solve_x_kernel(second_done, through, table, solved, residual, tips, work, work_through):
    zero = jnp.zeros((16, NZ), jnp.float32)
    for block in range(4):
        span = slice(block * 16, block * 16 + 16)

        def forward(i, carry):
            value, whole, ratio = carry
            value = second_done[i, span, :] + ratio * value
            whole = through[i, span, :] + ratio * whole
            work[i] = value
            work_through[i] = whole
            return value, whole, table[4, pl.ds(i, 1), :]

        lax.fori_loop(0, NX, forward, (zero, zero, jnp.zeros((1, NZ), jnp.float32)), unroll=32)

        def backward(step, carry):
            i = NX - 1 - step
            value, whole = carry
            inverse, ratio = table[5, pl.ds(i, 1), :], table[4, pl.ds(i, 1), :]
            value = inverse * work[i] + ratio * value
            whole = inverse * work_through[i] + ratio * whole
            solved[i, span, :] = value
            residual[i, span, :] = (second_done[i, span, :] - value) + (whole - value)
            if block == 0:
                tips[0, pl.ds(i, 1), :] = value[0:1]
            if block == 3:
                tips[1, pl.ds(i, 1), :] = value[15:16]
            return value, whole

        lax.fori_loop(0, NX, backward, (zero, zero), unroll=32)


def middle_kernel(*refs):
    parts = refs[:4]
    own, thick_high, thick_low, second_matrix, tips, table, spikes = refs[4:11]
    out, through, second = refs[11:14]
    scratch = refs[14:17]
    halo = refs[17]
    unused, unused, p, n = chain(4, place_on("gx", 2, 3), parts, DATA_X, *scratch)
    p, n = p[:DATA_X], n[:DATA_X]
    for side in range(2):
        halo[side] = (
            own[side, :DATA_X, :]
            + own[side, DATA_X : DATA_X + 1, :] * p
            + own[side, DATA_X + 1 : DATA_X + 2, :] * n
        )
    through[...] = times_thick(
        halo[...].reshape(2 * NY, NZ), thick_high, thick_low
    ).reshape(2, NY, NZ)
    for side in range(2):
        second[side] = times_second(second_matrix, through[side])
    for end in range(2):
        y = end * (NY - 1)
        prev_row, next_row = second[0, y : y + 1, :], second[1, y : y + 1, :]
        out[end, :NX, :] = tips[end] + table[0] * prev_row + table[1] * next_row
        row = lax.broadcasted_iota(jnp.int32, (8, NZ), 0)
        left, right = spikes[0, y : y + 1, :], spikes[1, y : y + 1, :]
        out[end, NX:, :] = jnp.where(
            row == 0,
            prev_row,
            jnp.where(row == 1, next_row, jnp.where(row == 2, left, jnp.where(row == 3, right, 0.0))),
        )


def lane_stencil(value, thick):
    lower, upper = pltpu.roll(value, 1, 1), pltpu.roll(value, NZ - 1, 1)
    return thick[2:3, :] * value - thick[3:4, :] * lower - thick[4:5, :] * upper


def local_kernel(
    solved, residual, temp, cure_adj, gain, cure_gain, second, halo_through, table, thick,
    base, cure_base,
):
    for block in range(4):
        span = slice(block * 16, block * 16 + 16)
        prev_value, next_value = second[0, span, :], second[1, span, :]
        prev_rest = halo_through[0, span, :] - 2.0 * prev_value
        next_rest = halo_through[1, span, :] - 2.0 * next_value

        @pl.loop(0, NX, unroll=16)
        def _(i):
            left, right = table[0, pl.ds(i, 1), :], table[1, pl.ds(i, 1), :]
            value = solved[i, span, :] + left * prev_value + right * next_value
            kick = residual[i, span, :] + left * prev_rest + right * next_rest
            kick = kick + lane_stencil(value, thick)
            lc = cure_adj[i, span, :]
            source = value + (cure_step / heat_release) * lc
            base[i, span, :] = temp[i, span, :] - explicit_part * kick + gain[i, span, :] * source
            cure_base[i, span, :] = lc + cure_gain[i, span, :] * source


def final_kernel(last, *refs):
    parts = refs[:4]
    own, base, gain, cure_base, cure_gain, spikes, table, thick = refs[4:12]
    outs = 2 if last else 3
    temp_out, cure_out = refs[12:14]
    rest = refs[12 + outs :]
    scratch, halo, kicks = rest[:3], rest[3], rest[4]
    unused, unused, p, n = chain(4, place_on("gy", 1, 3), parts, DATA_Y, *scratch)
    for side in range(2):
        value = (
            own[side]
            + own[side, DATA_Y : DATA_Y + 1, :] * p
            + own[side, DATA_Y + 1 : DATA_Y + 2, :] * n
        )
        halo[side, 8:40, :] = value[:NX]
        halo[side, 7:8, :] = value[NX : NX + 1]
        halo[side, 40:41, :] = value[NX + 1 : NX + 2]
        here = value[:NX]
        lower, upper = halo[side, 7:39, :], halo[side, 9:41, :]
        kick = table[2] * (here - lower) + table[3] * (here - upper)
        kicks[side] = -explicit_part * (kick + lane_stencil(here, thick))
    if last:
        temp_buffer, cure_buffer, sems = rest[5:8]
    copies = []
    for block in range(4):
        span = slice(block * 16, block * 16 + 16)
        left, right = spikes[0, span, :], spikes[1, span, :]

        def step(i, carry):
            delta = left * halo[0, pl.ds(i + 8, 1), :] + right * halo[1, pl.ds(i + 8, 1), :]
            kick = left * kicks[0, pl.ds(i, 1), :] + right * kicks[1, pl.ds(i, 1), :]
            value = base[i, span, :] + (gain[i, span, :] + explicit_part) * delta + kick
            cure_value = cure_base[i, span, :] + cure_gain[i, span, :] * delta
            if last:
                temp_buffer[block, i] = value
                cure_buffer[block, i] = cure_value
                return carry
            temp_out[i, span, :] = value
            cure_out[i, span, :] = cure_value
            low, high = carry
            low = low + table[6, pl.ds(i, 1), :] * value
            return low, high + table[7, pl.ds(i, 1), :] * value

        zero = jnp.zeros((16, NZ), jnp.float32)
        carry = lax.fori_loop(0, NX, step, () if last else (zero, zero), unroll=32)
        if last:
            for buffer, out, sem in (
                (temp_buffer, temp_out, sems.at[block, 0]),
                (cure_buffer, cure_out, sems.at[block, 1]),
            ):
                copy = pltpu.make_async_copy(buffer.at[block], out.at[:, span, :], sem)
                copy.start()
                copies.append(copy)
        else:
            refs[14][0, span, :] = carry[0]
            refs[14][1, span, :] = carry[1]
    for copy in copies:
        copy.wait()
    if not last:
        for end, i in ((0, 0), (1, NX - 1)):
            end_rows(
                refs[14], end, DATA_X, table[0, i : i + 1, :], table[1, i : i + 1, :]
            )


def exchange(message, axis, count, index):
    size = lax.axis_size(axis)
    at = {index(device): device for device in range(size)}
    received = [message]
    for mask in (1,) if count == 2 else (2, 3, 1):
        move = [(at[(rest, here)], at[(rest, here ^ mask)]) for rest, here in at]
        received.append(lax.ppermute(message, axis, move))
    return received


def along_z(device):
    return device // 4, device % 4


def along_y(device):
    return device % 4, device // 4


def along_core(device):
    return device // 2, device % 2


def along_x(device):
    return device % 2, device // 2


def per_device(
    temper_start,
    cure_start,
    temper_middle,
    cure_middle,
    adjoint_temper,
    adjoint_cure,
    conduct_first,
    inverse_first,
    conduct_second,
    inverse_second,
    conduct_thick,
    inverse_thick,
):
    hbm = pl.BlockSpec(memory_space=pltpu.HBM)
    (tips,) = call(
        tips_kernel,
        "tips",
        (adjoint_temper, inverse_first, conduct_first),
        (hbm, hbm, hbm),
        [f32(2, ROWS_X, NZ)],
        [
            pltpu.SMEM((NX, NX), jnp.float32),
            pltpu.SMEM((NX + 1,), jnp.float32),
            pltpu.VMEM((NX, NY, NZ), jnp.float32),
            pltpu.SemaphoreType.DMA((6,)),
        ],
        limit=65400000,
    )
    temp, cure_adj = adjoint_temper, adjoint_cure
    thick_high, thick_low = call(
        prepare_thick_kernel,
        "prepare_thick",
        (inverse_thick,),
        (vmem,),
        [bf16(NZ, NZ), bf16(NZ, NZ)],
    )
    fields = ((temper_middle, cure_middle), (temper_start, cure_start))
    for number, (temper, cure) in enumerate(fields):
        last = number == 1
        ring = exchange(tips, "gx", 4, along_z)
        (through,) = call(
            solve_z_kernel,
            "solve_z",
            (temp, thick_high, thick_low),
            [vmem] * 3,
            [f32(NX, NY, NZ)],
            flops=int(1.6e9),
        )
        gain, cure_gain = call(
            rates_kernel,
            "rates",
            (temper, cure, tips),
            [vmem, vmem, anywhere],
            [f32(NX, NY, NZ)] * 2,
            flops=int(1e9),
        )
        tips, own = call(
            functools.partial(chain_kernel, 4, DATA_X, ("gx", 0, 3)),
            "chain_z",
            (*ring, gain) if last else ring,
            [vmem] * 4 + ([anywhere] if last else []),
            [f32(2, ROWS_X, NZ)] * 2,
            chain_scratch(4, ROWS_X),
        )
        ring = exchange(tips, "gx", 4, along_y)
        if not last:
            table, spikes, second_matrix, thick = call(
                prepare_kernel,
                "prepare",
                (
                    inverse_first,
                    conduct_first,
                    inverse_second,
                    conduct_second,
                    inverse_second,
                    conduct_thick,
                    own,
                ),
                (*[smem] * 4, *[vmem] * 2, anywhere),
                [f32(8, NX, NZ), f32(2, NY, NZ), bf16(NY, 3 * NY), f32(8, NZ)],
            )
        (second_done,) = call(
            solve_y_kernel,
            "solve_y",
            (through, second_matrix),
            [vmem] * 2,
            [f32(NX, NY, NZ)],
            flops=int(1.6e9),
        )
        solved, residual, second_tips = call(
            solve_x_kernel,
            "solve_x",
            (second_done, through, table),
            [vmem] * 3,
            [f32(NX, NY, NZ), f32(NX, NY, NZ), f32(2, NX, NZ)],
            [pltpu.VMEM((NX, 16, NZ), jnp.float32)] * 2,
            flops=int(1e9),
        )
        message, halo_through, halo_second = call(
            middle_kernel,
            "middle",
            (*ring, own, thick_high, thick_low, second_matrix, second_tips, table, spikes),
            [vmem] * 11,
            [f32(2, ROWS_Y, NZ), f32(2, NY, NZ), f32(2, NY, NZ)],
            chain_scratch(4, ROWS_X) + [pltpu.VMEM((2, NY, NZ), jnp.float32)],
        )
        pair = exchange(message, "gy", 2, along_core)
        message, own = call(
            functools.partial(chain_kernel, 2, DATA_Y, ("gy", 0, 1)),
            "chain_core",
            pair,
            [vmem] * 2,
            [f32(2, ROWS_Y, NZ)] * 2,
            chain_scratch(2, ROWS_Y),
        )
        ring = exchange(message, "gy", 4, along_x)
        base, cure_base = call(
            local_kernel,
            "local",
            (solved, residual, temp, cure_adj, gain, cure_gain, halo_second, halo_through, table, thick),
            [vmem] * 10,
            [f32(NX, NY, NZ)] * 2,
            flops=int(1.6e9),
            limit=20 * MIB,
        )
        outs = [f32(NX, NY, NZ)] * 2 + ([] if last else [f32(2, ROWS_X, NZ)])
        buffers = [pltpu.VMEM((4, NX, 16, NZ), jnp.float32)] * 2 + [pltpu.SemaphoreType.DMA((4, 2))]
        results = call(
            functools.partial(final_kernel, last),
            "final",
            (*ring, own, base, gain, cure_base, cure_gain, spikes, table, thick),
            [vmem] * 12,
            outs,
            chain_scratch(4, ROWS_Y)
            + [pltpu.VMEM((2, 48, NZ), jnp.float32), pltpu.VMEM((2, NX, NZ), jnp.float32)]
            + (buffers if last else []),
            limit=20 * MIB,
            out_space=pl.BlockSpec(memory_space=pl.ANY) if last else vmem,
        )
        temp, cure_adj = results[0], results[1]
        if not last:
            tips = results[2]
    return (temp, cure_adj)


def solution(mesh):
    placed = (
        P("gx", "gy", None),
        P("gx", "gy", None),
        P("gx", "gy", None),
        P("gx", "gy", None),
        P("gx", "gy", None),
        P("gx", "gy", None),
        P("gx"),
        P("gx", None),
        P("gy"),
        P("gy", None),
        P(),
        P(),
    )
    return jax.shard_map(
        per_device,
        mesh=mesh,
        in_specs=placed,
        out_specs=(P("gx", "gy", None), P("gx", "gy", None)),
        check_vma=False,
    )
```

```python
import functools

import jax
import jax.numpy as jnp
from jax import lax
from jax.experimental import pallas as pl
from jax.experimental.pallas import tpu as pltpu
from jax.sharding import PartitionSpec as P

explicit_part = 2.0
heat_release = 100.0
cure_step = 0.5
arrhenius = 0.5
initial_rate = 0.1
highest = lax.Precision.HIGHEST

NX, NY, NZ = 32, 64, 256
ROWS_X, ROWS_Y = 72, 40
MASKS, LISTED = (2, 3, 1), (1, 3, 2)
DATA_X, DATA_Y = 64, 34
MIB = 1024 * 1024


vmem = pl.BlockSpec(memory_space=pltpu.VMEM)
smem = pl.BlockSpec(memory_space=pltpu.SMEM)
anywhere = pl.BlockSpec(memory_space=pl.ANY)


def f32(*shape):
    return jax.ShapeDtypeStruct(shape, jnp.float32)


def bf16(*shape):
    return jax.ShapeDtypeStruct(shape, jnp.bfloat16)


def call(kernel, name, operands, in_specs, outs, scratch=(), flops=0, limit=12 * MIB, out_space=vmem):
    size = sum(x.size * 4 for x in operands) + sum(o.size * 4 for o in outs)
    return pl.pallas_call(
        kernel,
        name=name,
        out_shape=tuple(outs),
        in_specs=list(in_specs),
        out_specs=tuple([out_space] * len(outs)),
        scratch_shapes=list(scratch),
        compiler_params=pltpu.CompilerParams(vmem_limit_bytes=limit),
        cost_estimate=pl.CostEstimate(flops=flops, bytes_accessed=size, transcendentals=0),
    )(*operands)


def place_on(axis, low, mask):
    return lax.bitwise_and(lax.shift_right_logical(lax.axis_index(axis), low), mask)


def chain(count, place, parts, data, gather, alphas, betas, keep=None):
    rows = gather.shape[2]
    masks = (0, 1) if count == 2 else (0, *MASKS)
    for mask, part in zip(masks, parts):
        gather[lax.bitwise_xor(place, mask)] = part[...]
    row = lax.broadcasted_iota(jnp.int32, (rows, NZ), 0)
    is_left, is_right = row == data, row == data + 1

    def source(j, end):
        value = gather[j, end]
        if j != 0:
            value = jnp.where(is_left, 0.0, value)
        if j != count - 1:
            value = jnp.where(is_right, 0.0, value)
        return value

    def coefficient(j, end, side):
        return gather[j, end, data + side : data + side + 1, :]

    first = [source(j, 0) for j in range(count)]
    last = [source(j, 1) for j in range(count)]
    left_first = [coefficient(j, 0, 0) for j in range(count)]
    left_last = [coefficient(j, 1, 0) for j in range(count)]
    right_first = [coefficient(j, 0, 1) for j in range(count)]
    right_last = [coefficient(j, 1, 1) for j in range(count)]

    pre, corner = [last[0]], [right_last[0]]
    forward, backward, both = [jnp.zeros_like(left_first[0])], {count - 1: jnp.zeros_like(left_first[0])}, []
    for t in range(1, count):
        inv = 1.0 / (1.0 - corner[-1] * left_first[t])
        gain = left_last[t] * inv
        forward.append(gain)
        pre.append(last[t] + gain * (pre[-1] + corner[-1] * first[t]))
        corner.append(right_last[t] + gain * corner[-1] * right_first[t])
    post, bend = {count - 1: first[-1]}, {count - 1: left_first[-1]}
    for t in range(count - 2, -1, -1):
        e, g = post[t + 1], bend[t + 1]
        gain = right_first[t] / (1.0 - g * right_last[t])
        backward[t] = gain
        post[t] = first[t] + gain * (e + g * last[t])
        bend[t] = left_first[t] + gain * g * left_last[t]
    alphas[0] = jnp.where(is_left, 1.0, jnp.zeros((rows, NZ), jnp.float32))
    betas[count - 1] = jnp.where(is_right, 1.0, jnp.zeros((rows, NZ), jnp.float32))
    for t in range(count - 1):
        a, c, e, g = pre[t], corner[t], post[t + 1], bend[t + 1]
        inv = 1.0 / (1.0 - c * g)
        alphas[t + 1] = (a + c * e) * inv
        betas[t] = (e + g * a) * inv
        both.append(inv)
    if keep is not None:
        both.append(jnp.zeros_like(both[0]))
        for t in range(count):
            from_right = forward[t] * corner[t - 1] if t else forward[0]
            from_left = backward[t] * bend[t + 1] if t < count - 1 else backward[t]
            rows_of = (corner[t], forward[t], bend[t], backward[t], both[t], from_right, from_left)
            for kind, value in enumerate(rows_of):
                keep[kind * count + t : kind * count + t + 1, :] = value
    return post[0], pre[-1], alphas[place], betas[place]


def kept(keep, kind, t):
    return keep[4 * kind + t : 4 * kind + t + 1, :]


def interfaces(place, pre, post, keep, alphas, betas):
    alphas[0] = jnp.zeros((NY, NZ), jnp.float32)
    betas[3] = jnp.zeros((NY, NZ), jnp.float32)
    for t in range(3):
        c, g, both = kept(keep, 0, t), kept(keep, 2, t + 1), kept(keep, 4, t)
        alphas[t + 1] = (pre[t] + c * post[t + 1]) * both
        betas[t] = (post[t + 1] + g * pre[t]) * both
    return alphas[place], betas[place]


def known_z_kernel(*refs):
    parts, keep, keep_next = refs[:4], refs[4], refs[5]
    messages, own, passed = refs[7:10], refs[10], refs[11]
    gather, alphas, betas = refs[12:15]
    place = place_on("gx", 0, 3)
    for mask, part in zip((0, *MASKS), parts):
        gather[lax.bitwise_xor(place, mask)] = part[...]
    first = [gather[j, 0] for j in range(4)]
    last = [gather[j, 1] for j in range(4)]
    pre, post = [last[0]], {3: first[3]}
    for t in range(1, 4):
        c, d = kept(keep, 0, t - 1), kept(keep, 1, t)
        pre.append(last[t] + d * (pre[-1] + c * first[t]))
    for t in range(2, -1, -1):
        g, e = kept(keep, 2, t + 1), kept(keep, 3, t)
        post[t] = first[t] + e * (post[t + 1] + g * last[t])
    alpha, beta = interfaces(place, pre, post, keep, alphas, betas)
    own[0] = alpha
    own[1] = beta
    line = place_on("gx", 2, 3)
    upwards = pre[3] + keep_next[pl.ds(20 + line, 1), :] * post[0]
    downwards = post[0] + keep_next[pl.ds(24 + line, 1), :] * pre[3]
    passed[0] = upwards
    passed[1] = downwards
    for mask, message in zip(LISTED, messages):
        message[...] = jnp.where(lax.bitwise_xor(line, mask) > line, upwards, downwards)


def known_y(parts, passed, keep, ups, downs, alphas, betas):
    line = place_on("gx", 2, 3)
    for mask, part in zip(LISTED, parts):
        place = lax.bitwise_xor(line, mask)
        value = part[...]
        ups[place] = value
        downs[place] = value
    ups[line] = passed[0]
    downs[line] = passed[1]
    pre, post = [ups[0]], {3: downs[3]}
    for t in range(1, 4):
        pre.append(ups[t] + kept(keep, 1, t) * pre[-1])
    for t in range(2, -1, -1):
        post[t] = downs[t] + kept(keep, 3, t) * post[t + 1]
    return interfaces(line, pre, post, keep, alphas, betas)


def chain_scratch(count, rows):
    return [
        pltpu.VMEM((count, 2, rows, NZ), jnp.float32),
        pltpu.VMEM((count, rows, NZ), jnp.float32),
        pltpu.VMEM((count, rows, NZ), jnp.float32),
    ]


def end_rows(out, end, start, left, right):
    row = lax.broadcasted_iota(jnp.int32, (8, NZ), 0)
    block = jnp.where(row == 0, left, jnp.where(row == 1, right, 0.0))
    out[end, start : start + 8, :] = block


def tips_kernel(field_hbm, inv_hbm, faces_hbm, out, inv, faces, field, sems):
    small = [
        pltpu.make_async_copy(inv_hbm, inv, sems.at[4]),
        pltpu.make_async_copy(faces_hbm, faces, sems.at[5]),
    ]
    large = []
    for block in range(4):
        span = slice(block * 16, block * 16 + 16)
        large.append(
            pltpu.make_async_copy(field_hbm.at[:, span, :], field.at[:, span, :], sems.at[block])
        )
    for copy in small + large:
        copy.start()
    for copy in small:
        copy.wait()
    for block in range(4):
        span = slice(block * 16, block * 16 + 16)
        large[block].wait()
        low = inv[0, 0] * field[0, span, :]
        high = inv[0, NX - 1] * field[0, span, :]
        for i in range(1, NX):
            value = field[i, span, :]
            low = low + inv[i, 0] * value
            high = high + inv[i, NX - 1] * value
        out[0, span, :] = low
        out[1, span, :] = high
    end_rows(out, 0, DATA_X, faces[0] * inv[0, 0], faces[NX] * inv[NX - 1, 0])
    end_rows(out, 1, DATA_X, faces[0] * inv[0, NX - 1], faces[NX] * inv[NX - 1, NX - 1])


def chain_kernel(count, data, place, *refs):
    parts, (tips, own), scratch = refs[:count], refs[count : count + 2], refs[-3:]
    keep = refs[count + 2] if len(refs) > count + 5 else None
    e, a, alpha, beta = chain(count, place_on(*place), parts, data, *scratch, keep)
    tips[0] = e
    tips[1] = a
    own[0] = alpha
    own[1] = beta


def split(value):
    high = value.astype(jnp.bfloat16)
    return high, (value - high.astype(jnp.float32)).astype(jnp.bfloat16)


def product(left, right):
    return jnp.dot(left, right, preferred_element_type=jnp.float32)


def times_thick(value, thick_high, thick_low):
    high, low = split(value)
    total = product(low, thick_high[...]) + product(high, thick_low[...])
    return total + product(high, thick_high[...])


def times_second(second, value):
    high, low = split(value)
    return product(second[...], jnp.concatenate([high, high, low], axis=0))


def prepare_thick_kernel(inverse_thick, thick_high, thick_low):
    thick_high[...], thick_low[...] = split(inverse_thick[...])


def prepare_kernel(
    inv, faces, inv_second, faces_second, inverse_t, thick, unused,
    table, spikes, second, thick_rows,
):
    def row(value):
        return jnp.full((1, NZ), value, jnp.float32)

    delta = row(1.0 + faces[0] + faces[1])
    for i in range(NX):
        table[0, i : i + 1, :] = row(faces[0] * inv[0, i])
        table[1, i : i + 1, :] = row(faces[NX] * inv[NX - 1, i])
        table[2, i : i + 1, :] = row(faces[i])
        table[3, i : i + 1, :] = row(faces[i + 1])
        table[6, i : i + 1, :] = row(inv[i, 0])
        table[7, i : i + 1, :] = row(inv[i, NX - 1])
        inverse = 1.0 / delta
        table[5, i : i + 1, :] = inverse
        ratio = faces[i + 1] * inverse
        table[4, i : i + 1, :] = ratio
        if i < NX - 1:
            delta = 1.0 + faces[i + 1] + faces[i + 2] - faces[i + 1] * ratio
    for y in range(NY):
        spikes[0, y : y + 1, :] = row(faces_second[0] * inv_second[0, y])
        spikes[1, y : y + 1, :] = row(faces_second[NY] * inv_second[NY - 1, y])
    high, low = split(inverse_t[...].T)
    second[...] = jnp.concatenate([high, low, high], axis=1)
    below = thick[0:NZ].reshape(1, NZ)
    above = thick[1 : NZ + 1].reshape(1, NZ)
    lane = lax.broadcasted_iota(jnp.int32, (1, NZ), 1)
    thick_rows[0:1, :] = below
    thick_rows[1:2, :] = above
    thick_rows[2:3, :] = below + above
    thick_rows[3:4, :] = jnp.where(lane == 0, 0.0, below)
    thick_rows[4:5, :] = jnp.where(lane == NZ - 1, 0.0, above)


def rates_kernel(temper, cure, unused, gain, cure_gain):
    @pl.loop(0, NX, unroll=2)
    def _(i):
        c = cure[i]
        heating = jnp.exp(arrhenius * temper[i])
        remain = 1.0 - c
        heated = heating * remain
        ready = initial_rate + c
        gain[i] = (heat_release * arrhenius) * (heated * ready * remain)
        cure_gain[i] = heat_release * (heated * (remain - 2.0 * ready))


def solve_z_kernel(field, thick_high, thick_low, out):
    @pl.loop(0, 8)
    def _(block):
        span = pl.ds(block * 4, 4)
        value = field[span].reshape(4 * NY, NZ)
        out[span] = times_thick(value, thick_high, thick_low).reshape(4, NY, NZ)


def solve_y_kernel(field, second, unused, out):
    @pl.loop(0, NX, unroll=4)
    def _(i):
        out[i] = times_second(second, field[i])


def solve_x_kernel(second_done, through, table, solved, residual, tips, work, work_through):
    zero = jnp.zeros((16, NZ), jnp.float32)
    for block in range(4):
        span = slice(block * 16, block * 16 + 16)

        def forward(i, carry):
            value, whole, ratio = carry
            value = second_done[i, span, :] + ratio * value
            whole = through[i, span, :] + ratio * whole
            work[i] = value
            work_through[i] = whole
            return value, whole, table[4, pl.ds(i, 1), :]

        lax.fori_loop(0, NX, forward, (zero, zero, jnp.zeros((1, NZ), jnp.float32)), unroll=32)

        def backward(step, carry):
            i = NX - 1 - step
            value, whole = carry
            inverse, ratio = table[5, pl.ds(i, 1), :], table[4, pl.ds(i, 1), :]
            value = inverse * work[i] + ratio * value
            whole = inverse * work_through[i] + ratio * whole
            solved[i, span, :] = value
            residual[i, span, :] = (second_done[i, span, :] - value) + (whole - value)
            if block == 0:
                tips[0, pl.ds(i, 1), :] = value[0:1]
            if block == 3:
                tips[1, pl.ds(i, 1), :] = value[15:16]
            return value, whole

        lax.fori_loop(0, NX, backward, (zero, zero), unroll=32)


def middle_kernel(last, *refs):
    if last:
        parts, passed, own, responses, keep = refs[:3], *refs[3:7]
        rest = refs[7:]
    else:
        parts, own = refs[:4], refs[4]
        responses, rest = own, refs[5:]
    thick_high, thick_low, second_matrix, tips, table, spikes, out, through, second = rest[:9]
    scratch, halo = rest[-4 - last : -1], rest[-1]
    if last:
        p, n = known_y(parts, passed, keep, *scratch)
    else:
        unused, unused, p, n = chain(4, place_on("gx", 2, 3), parts, DATA_X, *scratch, rest[9])
        p, n = p[:DATA_X], n[:DATA_X]
    for side in range(2):
        halo[side] = (
            own[side, :DATA_X, :]
            + responses[side, DATA_X : DATA_X + 1, :] * p
            + responses[side, DATA_X + 1 : DATA_X + 2, :] * n
        )
    through[...] = times_thick(
        halo[...].reshape(2 * NY, NZ), thick_high, thick_low
    ).reshape(2, NY, NZ)
    for side in range(2):
        second[side] = times_second(second_matrix, through[side])
    for end in range(2):
        y = end * (NY - 1)
        prev_row, next_row = second[0, y : y + 1, :], second[1, y : y + 1, :]
        out[end, :NX, :] = tips[end] + table[0] * prev_row + table[1] * next_row
        row = lax.broadcasted_iota(jnp.int32, (8, NZ), 0)
        left, right = spikes[0, y : y + 1, :], spikes[1, y : y + 1, :]
        out[end, NX:, :] = jnp.where(
            row == 0,
            prev_row,
            jnp.where(row == 1, next_row, jnp.where(row == 2, left, jnp.where(row == 3, right, 0.0))),
        )


def lane_stencil(value, thick):
    lower, upper = pltpu.roll(value, 1, 1), pltpu.roll(value, NZ - 1, 1)
    return thick[2:3, :] * value - thick[3:4, :] * lower - thick[4:5, :] * upper


def local_kernel(
    solved, residual, temp, cure_adj, gain, cure_gain, second, halo_through, table, thick,
    base, cure_base,
):
    for block in range(4):
        span = slice(block * 16, block * 16 + 16)
        prev_value, next_value = second[0, span, :], second[1, span, :]
        prev_rest = halo_through[0, span, :] - 2.0 * prev_value
        next_rest = halo_through[1, span, :] - 2.0 * next_value

        @pl.loop(0, NX, unroll=16)
        def _(i):
            left, right = table[0, pl.ds(i, 1), :], table[1, pl.ds(i, 1), :]
            value = solved[i, span, :] + left * prev_value + right * next_value
            kick = residual[i, span, :] + left * prev_rest + right * next_rest
            kick = kick + lane_stencil(value, thick)
            lc = cure_adj[i, span, :]
            source = value + (cure_step / heat_release) * lc
            base[i, span, :] = temp[i, span, :] - explicit_part * kick + gain[i, span, :] * source
            cure_base[i, span, :] = lc + cure_gain[i, span, :] * source


def final_kernel(last, *refs):
    parts = refs[:4]
    own, base, gain, cure_base, cure_gain, spikes, table, thick = refs[4:12]
    outs = 2 if last else 3
    temp_out, cure_out = refs[12:14]
    rest = refs[12 + outs :]
    scratch, halo, kicks = rest[:3], rest[3], rest[4]
    unused, unused, p, n = chain(4, place_on("gy", 1, 3), parts, DATA_Y, *scratch)
    for side in range(2):
        value = (
            own[side]
            + own[side, DATA_Y : DATA_Y + 1, :] * p
            + own[side, DATA_Y + 1 : DATA_Y + 2, :] * n
        )
        halo[side, 8:40, :] = value[:NX]
        halo[side, 7:8, :] = value[NX : NX + 1]
        halo[side, 40:41, :] = value[NX + 1 : NX + 2]
        here = value[:NX]
        lower, upper = halo[side, 7:39, :], halo[side, 9:41, :]
        kick = table[2] * (here - lower) + table[3] * (here - upper)
        kicks[side] = -explicit_part * (kick + lane_stencil(here, thick))
    if last:
        temp_buffer, cure_buffer, sems = rest[5:8]
    copies = []
    for block in range(4):
        span = slice(block * 16, block * 16 + 16)
        left, right = spikes[0, span, :], spikes[1, span, :]

        def step(i, carry):
            delta = left * halo[0, pl.ds(i + 8, 1), :] + right * halo[1, pl.ds(i + 8, 1), :]
            kick = left * kicks[0, pl.ds(i, 1), :] + right * kicks[1, pl.ds(i, 1), :]
            value = base[i, span, :] + (gain[i, span, :] + explicit_part) * delta + kick
            cure_value = cure_base[i, span, :] + cure_gain[i, span, :] * delta
            if last:
                temp_buffer[block, i] = value
                cure_buffer[block, i] = cure_value
                return carry
            temp_out[i, span, :] = value
            cure_out[i, span, :] = cure_value
            low, high = carry
            low = low + table[6, pl.ds(i, 1), :] * value
            return low, high + table[7, pl.ds(i, 1), :] * value

        zero = jnp.zeros((16, NZ), jnp.float32)
        carry = lax.fori_loop(0, NX, step, () if last else (zero, zero), unroll=32)
        if last:
            for buffer, out, sem in (
                (temp_buffer, temp_out, sems.at[block, 0]),
                (cure_buffer, cure_out, sems.at[block, 1]),
            ):
                copy = pltpu.make_async_copy(buffer.at[block], out.at[:, span, :], sem)
                copy.start()
                copies.append(copy)
        else:
            refs[14][0, span, :] = carry[0]
            refs[14][1, span, :] = carry[1]
    for copy in copies:
        copy.wait()


def exchange(message, axis, count, index):
    size = lax.axis_size(axis)
    at = {index(device): device for device in range(size)}
    several = isinstance(message, list)
    received = [] if several else [message]
    for number, mask in enumerate((1,) if count == 2 else LISTED if several else MASKS):
        move = [(at[(rest, here)], at[(rest, here ^ mask)]) for rest, here in at]
        received.append(lax.ppermute(message[number] if several else message, axis, move))
    return received


def along_z(device):
    return device // 4, device % 4


def along_y(device):
    return device % 4, device // 4


def along_core(device):
    return device // 2, device % 2


def along_x(device):
    return device % 2, device // 2


def per_device(
    temper_start,
    cure_start,
    temper_middle,
    cure_middle,
    adjoint_temper,
    adjoint_cure,
    conduct_first,
    inverse_first,
    conduct_second,
    inverse_second,
    conduct_thick,
    inverse_thick,
):
    hbm = pl.BlockSpec(memory_space=pltpu.HBM)
    (tips,) = call(
        tips_kernel,
        "tips",
        (adjoint_temper, inverse_first, conduct_first),
        (hbm, hbm, hbm),
        [f32(2, ROWS_X, NZ)],
        [
            pltpu.SMEM((NX, NX), jnp.float32),
            pltpu.SMEM((NX + 1,), jnp.float32),
            pltpu.VMEM((NX, NY, NZ), jnp.float32),
            pltpu.SemaphoreType.DMA((6,)),
        ],
        limit=65400000,
    )
    temp, cure_adj = adjoint_temper, adjoint_cure
    thick_high, thick_low = call(
        prepare_thick_kernel,
        "prepare_thick",
        (inverse_thick,),
        (vmem,),
        [bf16(NZ, NZ), bf16(NZ, NZ)],
    )
    fields = ((temper_middle, cure_middle), (temper_start, cure_start))
    for number, (temper, cure) in enumerate(fields):
        last = number == 1
        ring = exchange(tips, "gx", 4, along_z)
        (through,) = call(
            solve_z_kernel,
            "solve_z",
            (temp, thick_high, thick_low),
            [vmem] * 3,
            [f32(NX, NY, NZ)],
            flops=int(1.6e9),
        )
        gain, cure_gain = call(
            rates_kernel,
            "rates",
            (temper, cure, tips),
            [vmem, vmem, anywhere],
            [f32(NX, NY, NZ)] * 2,
            flops=int(1e9),
        )
        if not last:
            tips, own, keep_z = call(
                functools.partial(chain_kernel, 4, DATA_X, ("gx", 0, 3)),
                "chain_z",
                ring,
                [vmem] * 4,
                [f32(2, ROWS_X, NZ), f32(2, ROWS_X, NZ), f32(32, NZ)],
                chain_scratch(4, ROWS_X),
            )
            responses = own
        else:
            *tips, own, passed = call(
                known_z_kernel,
                "chain_z",
                (*ring, keep_z, keep_y, gain),
                [vmem] * 6 + [anywhere],
                [f32(NY, NZ)] * 3 + [f32(2, NY, NZ)] * 2,
                chain_scratch(4, NY),
            )
        ring = exchange(tips, "gx", 4, along_y)
        if not last:
            table, spikes, second_matrix, thick = call(
                prepare_kernel,
                "prepare",
                (
                    inverse_first,
                    conduct_first,
                    inverse_second,
                    conduct_second,
                    inverse_second,
                    conduct_thick,
                    own,
                ),
                (*[smem] * 4, *[vmem] * 2, anywhere),
                [f32(8, NX, NZ), f32(2, NY, NZ), bf16(NY, 3 * NY), f32(8, NZ)],
            )
        (second_done,) = call(
            solve_y_kernel,
            "solve_y",
            (through, second_matrix, own),
            [vmem, vmem, anywhere],
            [f32(NX, NY, NZ)],
            flops=int(1.6e9),
        )
        solved, residual, second_tips = call(
            solve_x_kernel,
            "solve_x",
            (second_done, through, table),
            [vmem] * 3,
            [f32(NX, NY, NZ), f32(NX, NY, NZ), f32(2, NX, NZ)],
            [pltpu.VMEM((NX, 16, NZ), jnp.float32)] * 2,
            flops=int(1e9),
        )
        outs = [f32(2, ROWS_Y, NZ), f32(2, NY, NZ), f32(2, NY, NZ)]
        known = (passed, own, responses, keep_y) if last else (own,)
        operands = (*ring, *known, thick_high, thick_low, second_matrix, second_tips, table, spikes)
        message, halo_through, halo_second, *more = call(
            functools.partial(middle_kernel, last),
            "middle",
            operands,
            [vmem] * len(operands),
            outs if last else outs + [f32(32, NZ)],
            ([pltpu.VMEM((4, NY, NZ), jnp.float32)] * 4 if last else chain_scratch(4, ROWS_X))
            + [pltpu.VMEM((2, NY, NZ), jnp.float32)],
        )
        if not last:
            (keep_y,) = more
        pair = exchange(message, "gy", 2, along_core)
        message, own = call(
            functools.partial(chain_kernel, 2, DATA_Y, ("gy", 0, 1)),
            "chain_core",
            pair,
            [vmem] * 2,
            [f32(2, ROWS_Y, NZ)] * 2,
            chain_scratch(2, ROWS_Y),
        )
        ring = exchange(message, "gy", 4, along_x)
        base, cure_base = call(
            local_kernel,
            "local",
            (solved, residual, temp, cure_adj, gain, cure_gain, halo_second, halo_through, table, thick),
            [vmem] * 10,
            [f32(NX, NY, NZ)] * 2,
            flops=int(1.6e9),
            limit=20 * MIB,
        )
        outs = [f32(NX, NY, NZ)] * 2 + ([] if last else [f32(2, NY, NZ)])
        buffers = [pltpu.VMEM((4, NX, 16, NZ), jnp.float32)] * 2 + [pltpu.SemaphoreType.DMA((4, 2))]
        results = call(
            functools.partial(final_kernel, last),
            "final",
            (*ring, own, base, gain, cure_base, cure_gain, spikes, table, thick),
            [vmem] * 12,
            outs,
            chain_scratch(4, ROWS_Y)
            + [pltpu.VMEM((2, 48, NZ), jnp.float32), pltpu.VMEM((2, NX, NZ), jnp.float32)]
            + (buffers if last else []),
            limit=20 * MIB,
            out_space=pl.BlockSpec(memory_space=pl.ANY) if last else vmem,
        )
        temp, cure_adj = results[0], results[1]
        if not last:
            tips = results[2]
    return (temp, cure_adj)


def solution(mesh):
    placed = (
        P("gx", "gy", None),
        P("gx", "gy", None),
        P("gx", "gy", None),
        P("gx", "gy", None),
        P("gx", "gy", None),
        P("gx", "gy", None),
        P("gx"),
        P("gx", None),
        P("gy"),
        P("gy", None),
        P(),
        P(),
    )
    return jax.shard_map(
        per_device,
        mesh=mesh,
        in_specs=placed,
        out_specs=(P("gx", "gy", None), P("gx", "gy", None)),
        check_vma=False,
    )
```

```python
import functools

import jax
import jax.numpy as jnp
from jax import lax
from jax.experimental import pallas as pl
from jax.experimental.pallas import tpu as pltpu
from jax.sharding import PartitionSpec as P

explicit_part = 2.0
heat_release = 100.0
cure_step = 0.5
arrhenius = 0.5
initial_rate = 0.1
highest = lax.Precision.HIGHEST

NX, NY, NZ = 32, 64, 256
ROWS_X, ROWS_Y = 72, 40
MASKS, LISTED = (2, 3, 1), (1, 3, 2)
DATA_X, DATA_Y = 64, 34
MIB = 1024 * 1024


vmem = pl.BlockSpec(memory_space=pltpu.VMEM)
smem = pl.BlockSpec(memory_space=pltpu.SMEM)
anywhere = pl.BlockSpec(memory_space=pl.ANY)


def f32(*shape):
    return jax.ShapeDtypeStruct(shape, jnp.float32)


def bf16(*shape):
    return jax.ShapeDtypeStruct(shape, jnp.bfloat16)


def call(kernel, name, operands, in_specs, outs, scratch=(), flops=0, limit=12 * MIB, out_space=vmem):
    size = sum(x.size * 4 for x in operands) + sum(o.size * 4 for o in outs)
    return pl.pallas_call(
        kernel,
        name=name,
        out_shape=tuple(outs),
        in_specs=list(in_specs),
        out_specs=tuple([out_space] * len(outs)),
        scratch_shapes=list(scratch),
        compiler_params=pltpu.CompilerParams(vmem_limit_bytes=limit),
        cost_estimate=pl.CostEstimate(flops=flops, bytes_accessed=size, transcendentals=0),
    )(*operands)


def place_on(axis, low, mask):
    return lax.bitwise_and(lax.shift_right_logical(lax.axis_index(axis), low), mask)


def chain(count, place, parts, data, gather, alphas, betas, keep=None):
    rows = gather.shape[2]
    masks = (0, 1) if count == 2 else (0, *MASKS)
    for mask, part in zip(masks, parts):
        gather[lax.bitwise_xor(place, mask)] = part[...]
    row = lax.broadcasted_iota(jnp.int32, (rows, NZ), 0)
    is_left, is_right = row == data, row == data + 1

    def source(j, end):
        value = gather[j, end]
        if j != 0:
            value = jnp.where(is_left, 0.0, value)
        if j != count - 1:
            value = jnp.where(is_right, 0.0, value)
        return value

    def coefficient(j, end, side):
        return gather[j, end, data + side : data + side + 1, :]

    first = [source(j, 0) for j in range(count)]
    last = [source(j, 1) for j in range(count)]
    left_first = [coefficient(j, 0, 0) for j in range(count)]
    left_last = [coefficient(j, 1, 0) for j in range(count)]
    right_first = [coefficient(j, 0, 1) for j in range(count)]
    right_last = [coefficient(j, 1, 1) for j in range(count)]

    pre, corner = [last[0]], [right_last[0]]
    forward, backward, both = [jnp.zeros_like(left_first[0])], {count - 1: jnp.zeros_like(left_first[0])}, []
    for t in range(1, count):
        inv = 1.0 / (1.0 - corner[-1] * left_first[t])
        gain = left_last[t] * inv
        forward.append(gain)
        pre.append(last[t] + gain * (pre[-1] + corner[-1] * first[t]))
        corner.append(right_last[t] + gain * corner[-1] * right_first[t])
    post, bend = {count - 1: first[-1]}, {count - 1: left_first[-1]}
    for t in range(count - 2, -1, -1):
        e, g = post[t + 1], bend[t + 1]
        gain = right_first[t] / (1.0 - g * right_last[t])
        backward[t] = gain
        post[t] = first[t] + gain * (e + g * last[t])
        bend[t] = left_first[t] + gain * g * left_last[t]
    alphas[0] = jnp.where(is_left, 1.0, jnp.zeros((rows, NZ), jnp.float32))
    betas[count - 1] = jnp.where(is_right, 1.0, jnp.zeros((rows, NZ), jnp.float32))
    for t in range(count - 1):
        a, c, e, g = pre[t], corner[t], post[t + 1], bend[t + 1]
        inv = 1.0 / (1.0 - c * g)
        alphas[t + 1] = (a + c * e) * inv
        betas[t] = (e + g * a) * inv
        both.append(inv)
    if keep is not None:
        both.append(jnp.zeros_like(both[0]))
        for t in range(count):
            from_right = forward[t] * corner[t - 1] if t else forward[0]
            from_left = backward[t] * bend[t + 1] if t < count - 1 else backward[t]
            rows_of = (corner[t], forward[t], bend[t], backward[t], both[t], from_right, from_left)
            for kind, value in enumerate(rows_of):
                keep[kind * count + t : kind * count + t + 1, :] = value
    return post[0], pre[-1], alphas[place], betas[place]


def kept(keep, kind, t):
    return keep[4 * kind + t : 4 * kind + t + 1, :]


def interfaces(place, pre, post, keep, alphas, betas):
    alphas[0] = jnp.zeros_like(pre[0])
    betas[3] = jnp.zeros_like(pre[0])
    for t in range(3):
        c, g, both = kept(keep, 0, t), kept(keep, 2, t + 1), kept(keep, 4, t)
        alphas[t + 1] = (pre[t] + c * post[t + 1]) * both
        betas[t] = (post[t + 1] + g * pre[t]) * both
    return alphas[place], betas[place]


def known_core_kernel(*refs):
    parts, keep, messages, own, passed = refs[:2], refs[2], refs[3:6], refs[6], refs[7]
    e, a, alpha, beta = chain(2, place_on("gy", 0, 1), parts, DATA_Y, *refs[8:11])
    own[0] = alpha
    own[1] = beta
    pass_on(place_on("gy", 1, 3), e, a, keep, messages, passed)


def known_z_kernel(*refs):
    parts, keep, keep_next = refs[:4], refs[4], refs[5]
    messages, own, passed = refs[7:10], refs[10], refs[11]
    gather, alphas, betas = refs[12:15]
    place = place_on("gx", 0, 3)
    for mask, part in zip((0, *MASKS), parts):
        gather[lax.bitwise_xor(place, mask)] = part[...]
    first = [gather[j, 0] for j in range(4)]
    last = [gather[j, 1] for j in range(4)]
    pre, post = [last[0]], {3: first[3]}
    for t in range(1, 4):
        c, d = kept(keep, 0, t - 1), kept(keep, 1, t)
        pre.append(last[t] + d * (pre[-1] + c * first[t]))
    for t in range(2, -1, -1):
        g, e = kept(keep, 2, t + 1), kept(keep, 3, t)
        post[t] = first[t] + e * (post[t + 1] + g * last[t])
    alpha, beta = interfaces(place, pre, post, keep, alphas, betas)
    own[0] = alpha
    own[1] = beta
    pass_on(place_on("gx", 2, 3), post[0], pre[3], keep_next, messages, passed)


def pass_on(line, first, last, keep, messages, passed):
    upwards = last + keep[pl.ds(20 + line, 1), :] * first
    downwards = first + keep[pl.ds(24 + line, 1), :] * last
    passed[0] = upwards
    passed[1] = downwards
    for mask, message in zip(LISTED, messages):
        message[...] = jnp.where(lax.bitwise_xor(line, mask) > line, upwards, downwards)


def known_line(line, parts, passed, keep, ups, downs, alphas, betas):
    for mask, part in zip(LISTED, parts):
        place = lax.bitwise_xor(line, mask)
        value = part[...]
        ups[place] = value
        downs[place] = value
    ups[line] = passed[0]
    downs[line] = passed[1]
    pre, post = [ups[0]], {3: downs[3]}
    for t in range(1, 4):
        pre.append(ups[t] + kept(keep, 1, t) * pre[-1])
    for t in range(2, -1, -1):
        post[t] = downs[t] + kept(keep, 3, t) * post[t + 1]
    return interfaces(line, pre, post, keep, alphas, betas)


def chain_scratch(count, rows):
    return [
        pltpu.VMEM((count, 2, rows, NZ), jnp.float32),
        pltpu.VMEM((count, rows, NZ), jnp.float32),
        pltpu.VMEM((count, rows, NZ), jnp.float32),
    ]


def end_rows(out, end, start, left, right):
    row = lax.broadcasted_iota(jnp.int32, (8, NZ), 0)
    block = jnp.where(row == 0, left, jnp.where(row == 1, right, 0.0))
    out[end, start : start + 8, :] = block


def tips_kernel(field_hbm, inv_hbm, faces_hbm, out, inv, faces, field, sems):
    small = [
        pltpu.make_async_copy(inv_hbm, inv, sems.at[8]),
        pltpu.make_async_copy(faces_hbm, faces, sems.at[9]),
    ]
    large = []
    for block in range(8):
        span = slice(block * 8, block * 8 + 8)
        large.append(
            pltpu.make_async_copy(field_hbm.at[:, span, :], field.at[:, span, :], sems.at[block])
        )
    for copy in small + large:
        copy.start()
    for copy in small:
        copy.wait()
    for block in range(8):
        span = slice(block * 8, block * 8 + 8)
        large[block].wait()
        low = inv[0, 0] * field[0, span, :]
        high = inv[0, NX - 1] * field[0, span, :]
        for i in range(1, NX):
            value = field[i, span, :]
            low = low + inv[i, 0] * value
            high = high + inv[i, NX - 1] * value
        out[0, span, :] = low
        out[1, span, :] = high
    end_rows(out, 0, DATA_X, faces[0] * inv[0, 0], faces[NX] * inv[NX - 1, 0])
    end_rows(out, 1, DATA_X, faces[0] * inv[0, NX - 1], faces[NX] * inv[NX - 1, NX - 1])


def chain_kernel(count, data, place, *refs):
    parts, (tips, own), scratch = refs[:count], refs[count : count + 2], refs[-3:]
    keep = refs[count + 2] if len(refs) > count + 5 else None
    e, a, alpha, beta = chain(count, place_on(*place), parts, data, *scratch, keep)
    tips[0] = e
    tips[1] = a
    own[0] = alpha
    own[1] = beta


def split(value):
    high = value.astype(jnp.bfloat16)
    return high, (value - high.astype(jnp.float32)).astype(jnp.bfloat16)


def product(left, right):
    return jnp.dot(left, right, preferred_element_type=jnp.float32)


def times_thick(value, thick_high, thick_low):
    high, low = split(value)
    total = product(low, thick_high[...]) + product(high, thick_low[...])
    return total + product(high, thick_high[...])


def times_second(second, value):
    high, low = split(value)
    return product(second[...], jnp.concatenate([high, high, low], axis=0))


def prepare_thick_kernel(inverse_thick, thick_high, thick_low):
    thick_high[...], thick_low[...] = split(inverse_thick[...])


def prepare_kernel(
    inv, faces, inv_second, faces_second, inverse_t, thick, unused,
    table, spikes, second, thick_rows,
):
    def row(value):
        return jnp.full((1, NZ), value, jnp.float32)

    delta = row(1.0 + faces[0] + faces[1])
    for i in range(NX):
        table[0, i : i + 1, :] = row(faces[0] * inv[0, i])
        table[1, i : i + 1, :] = row(faces[NX] * inv[NX - 1, i])
        table[2, i : i + 1, :] = row(faces[i])
        table[3, i : i + 1, :] = row(faces[i + 1])
        table[6, i : i + 1, :] = row(inv[i, 0])
        table[7, i : i + 1, :] = row(inv[i, NX - 1])
        inverse = 1.0 / delta
        table[5, i : i + 1, :] = inverse
        ratio = faces[i + 1] * inverse
        table[4, i : i + 1, :] = ratio
        if i < NX - 1:
            delta = 1.0 + faces[i + 1] + faces[i + 2] - faces[i + 1] * ratio
    for y in range(NY):
        spikes[0, y : y + 1, :] = row(faces_second[0] * inv_second[0, y])
        spikes[1, y : y + 1, :] = row(faces_second[NY] * inv_second[NY - 1, y])
    high, low = split(inverse_t[...].T)
    second[...] = jnp.concatenate([high, low, high], axis=1)
    below = thick[0:NZ].reshape(1, NZ)
    above = thick[1 : NZ + 1].reshape(1, NZ)
    lane = lax.broadcasted_iota(jnp.int32, (1, NZ), 1)
    thick_rows[0:1, :] = below
    thick_rows[1:2, :] = above
    thick_rows[2:3, :] = below + above
    thick_rows[3:4, :] = jnp.where(lane == 0, 0.0, below)
    thick_rows[4:5, :] = jnp.where(lane == NZ - 1, 0.0, above)


def rates_kernel(temper, cure, unused, gain, cure_gain):
    @pl.loop(0, NX, unroll=2)
    def _(i):
        c = cure[i]
        heating = jnp.exp(arrhenius * temper[i])
        remain = 1.0 - c
        heated = heating * remain
        ready = initial_rate + c
        gain[i] = (heat_release * arrhenius) * (heated * ready * remain)
        cure_gain[i] = heat_release * (heated * (remain - 2.0 * ready))


def solve_z_kernel(field, thick_high, thick_low, out):
    @pl.loop(0, 8)
    def _(block):
        span = pl.ds(block * 4, 4)
        value = field[span].reshape(4 * NY, NZ)
        out[span] = times_thick(value, thick_high, thick_low).reshape(4, NY, NZ)


def solve_y_kernel(field, second, unused, out):
    @pl.loop(0, NX, unroll=4)
    def _(i):
        out[i] = times_second(second, field[i])


def solve_x_kernel(second_done, through, table, solved, residual, tips, work, work_through):
    zero = jnp.zeros((16, NZ), jnp.float32)
    for block in range(4):
        span = slice(block * 16, block * 16 + 16)

        def forward(i, carry):
            value, whole, ratio = carry
            value = second_done[i, span, :] + ratio * value
            whole = through[i, span, :] + ratio * whole
            work[i] = value
            work_through[i] = whole
            return value, whole, table[4, pl.ds(i, 1), :]

        lax.fori_loop(0, NX, forward, (zero, zero, jnp.zeros((1, NZ), jnp.float32)), unroll=32)

        def backward(step, carry):
            i = NX - 1 - step
            value, whole = carry
            inverse, ratio = table[5, pl.ds(i, 1), :], table[4, pl.ds(i, 1), :]
            value = inverse * work[i] + ratio * value
            whole = inverse * work_through[i] + ratio * whole
            solved[i, span, :] = value
            residual[i, span, :] = (second_done[i, span, :] - value) + (whole - value)
            if block == 0:
                tips[0, pl.ds(i, 1), :] = value[0:1]
            if block == 3:
                tips[1, pl.ds(i, 1), :] = value[15:16]
            return value, whole

        lax.fori_loop(0, NX, backward, (zero, zero), unroll=32)


def middle_kernel(last, *refs):
    if last:
        parts, passed, own, responses, keep = refs[:3], *refs[3:7]
        rest = refs[7:]
    else:
        parts, own = refs[:4], refs[4]
        responses, rest = own, refs[5:]
    thick_high, thick_low, second_matrix, tips, table, spikes, out, through, second = rest[:9]
    scratch, halo = rest[-4 - last : -1], rest[-1]
    if last:
        p, n = known_line(place_on("gx", 2, 3), parts, passed, keep, *scratch)
    else:
        unused, unused, p, n = chain(4, place_on("gx", 2, 3), parts, DATA_X, *scratch, rest[9])
        p, n = p[:DATA_X], n[:DATA_X]
    for side in range(2):
        halo[side] = (
            own[side, :DATA_X, :]
            + responses[side, DATA_X : DATA_X + 1, :] * p
            + responses[side, DATA_X + 1 : DATA_X + 2, :] * n
        )
    through[...] = times_thick(
        halo[...].reshape(2 * NY, NZ), thick_high, thick_low
    ).reshape(2, NY, NZ)
    for side in range(2):
        second[side] = times_second(second_matrix, through[side])
    for end in range(2):
        y = end * (NY - 1)
        prev_row, next_row = second[0, y : y + 1, :], second[1, y : y + 1, :]
        out[end, :NX, :] = tips[end] + table[0] * prev_row + table[1] * next_row
        row = lax.broadcasted_iota(jnp.int32, (8, NZ), 0)
        left, right = spikes[0, y : y + 1, :], spikes[1, y : y + 1, :]
        out[end, NX:, :] = jnp.where(
            row == 0,
            prev_row,
            jnp.where(row == 1, next_row, jnp.where(row == 2, left, jnp.where(row == 3, right, 0.0))),
        )


def lane_stencil(value, thick):
    lower, upper = pltpu.roll(value, 1, 1), pltpu.roll(value, NZ - 1, 1)
    return thick[2:3, :] * value - thick[3:4, :] * lower - thick[4:5, :] * upper


def local_kernel(
    solved, residual, temp, cure_adj, gain, cure_gain, second, halo_through, table, thick,
    base, cure_base,
):
    for block in range(4):
        span = slice(block * 16, block * 16 + 16)
        prev_value, next_value = second[0, span, :], second[1, span, :]
        prev_rest = halo_through[0, span, :] - 2.0 * prev_value
        next_rest = halo_through[1, span, :] - 2.0 * next_value

        @pl.loop(0, NX, unroll=16)
        def _(i):
            left, right = table[0, pl.ds(i, 1), :], table[1, pl.ds(i, 1), :]
            value = solved[i, span, :] + left * prev_value + right * next_value
            kick = residual[i, span, :] + left * prev_rest + right * next_rest
            kick = kick + lane_stencil(value, thick)
            lc = cure_adj[i, span, :]
            source = value + (cure_step / heat_release) * lc
            base[i, span, :] = temp[i, span, :] - explicit_part * kick + gain[i, span, :] * source
            cure_base[i, span, :] = lc + cure_gain[i, span, :] * source


def final_kernel(last, *refs):
    count = 5 if last else 4
    parts, tail = refs[:count], refs[count:]
    own, base, gain, cure_base, cure_gain, spikes, table, thick, temp_out, cure_out = tail[:10]
    if last:
        scratch, rest = tail[10:14], tail[14:]
        p, n = known_line(place_on("gy", 1, 3), parts[:3], parts[3], parts[4], *scratch)
    else:
        tips, keep = tail[10:12]
        scratch, rest = tail[12:15], tail[15:]
        unused, unused, p, n = chain(4, place_on("gy", 1, 3), parts, DATA_Y, *scratch, keep)
    halo, kicks = rest[:2]
    for side in range(2):
        value = (
            own[side]
            + own[side, DATA_Y : DATA_Y + 1, :] * p
            + own[side, DATA_Y + 1 : DATA_Y + 2, :] * n
        )
        halo[side, 8:40, :] = value[:NX]
        halo[side, 7:8, :] = value[NX : NX + 1]
        halo[side, 40:41, :] = value[NX + 1 : NX + 2]
        here = value[:NX]
        lower, upper = halo[side, 7:39, :], halo[side, 9:41, :]
        kick = table[2] * (here - lower) + table[3] * (here - upper)
        kicks[side] = -explicit_part * (kick + lane_stencil(here, thick))
    if last:
        temp_buffer, cure_buffer, sems = rest[2:5]
    copies = []
    for block in range(4):
        span = slice(block * 16, block * 16 + 16)
        left, right = spikes[0, span, :], spikes[1, span, :]

        def step(i, carry):
            delta = left * halo[0, pl.ds(i + 8, 1), :] + right * halo[1, pl.ds(i + 8, 1), :]
            kick = left * kicks[0, pl.ds(i, 1), :] + right * kicks[1, pl.ds(i, 1), :]
            value = base[i, span, :] + (gain[i, span, :] + explicit_part) * delta + kick
            cure_value = cure_base[i, span, :] + cure_gain[i, span, :] * delta
            if last:
                temp_buffer[block, i] = value
                cure_buffer[block, i] = cure_value
                return carry
            temp_out[i, span, :] = value
            cure_out[i, span, :] = cure_value
            low, high = carry
            low = low + table[6, pl.ds(i, 1), :] * value
            return low, high + table[7, pl.ds(i, 1), :] * value

        zero = jnp.zeros((16, NZ), jnp.float32)
        carry = lax.fori_loop(0, NX, step, () if last else (zero, zero), unroll=32)
        if last:
            for buffer, out, sem in (
                (temp_buffer, temp_out, sems.at[block, 0]),
                (cure_buffer, cure_out, sems.at[block, 1]),
            ):
                copy = pltpu.make_async_copy(buffer.at[block], out.at[:, span, :], sem)
                copy.start()
                copies.append(copy)
        else:
            tips[0, span, :] = carry[0]
            tips[1, span, :] = carry[1]
    for copy in copies:
        copy.wait()


def exchange(message, axis, count, index):
    size = lax.axis_size(axis)
    at = {index(device): device for device in range(size)}
    several = isinstance(message, list)
    received = [] if several else [message]
    for number, mask in enumerate((1,) if count == 2 else LISTED if several else MASKS):
        move = [(at[(rest, here)], at[(rest, here ^ mask)]) for rest, here in at]
        received.append(lax.ppermute(message[number] if several else message, axis, move))
    return received


def along_z(device):
    return device // 4, device % 4


def along_y(device):
    return device % 4, device // 4


def along_core(device):
    return device // 2, device % 2


def along_x(device):
    return device % 2, device // 2


def per_device(
    temper_start,
    cure_start,
    temper_middle,
    cure_middle,
    adjoint_temper,
    adjoint_cure,
    conduct_first,
    inverse_first,
    conduct_second,
    inverse_second,
    conduct_thick,
    inverse_thick,
):
    hbm = pl.BlockSpec(memory_space=pltpu.HBM)
    (tips,) = call(
        tips_kernel,
        "tips",
        (adjoint_temper, inverse_first, conduct_first),
        (hbm, hbm, hbm),
        [f32(2, ROWS_X, NZ)],
        [
            pltpu.SMEM((NX, NX), jnp.float32),
            pltpu.SMEM((NX + 1,), jnp.float32),
            pltpu.VMEM((NX, NY, NZ), jnp.float32),
            pltpu.SemaphoreType.DMA((10,)),
        ],
        limit=65400000,
    )
    temp, cure_adj = adjoint_temper, adjoint_cure
    thick_high, thick_low = call(
        prepare_thick_kernel,
        "prepare_thick",
        (inverse_thick,),
        (vmem,),
        [bf16(NZ, NZ), bf16(NZ, NZ)],
    )
    fields = ((temper_middle, cure_middle), (temper_start, cure_start))
    for number, (temper, cure) in enumerate(fields):
        last = number == 1
        ring = exchange(tips, "gx", 4, along_z)
        (through,) = call(
            solve_z_kernel,
            "solve_z",
            (temp, thick_high, thick_low),
            [vmem] * 3,
            [f32(NX, NY, NZ)],
            flops=int(1.6e9),
        )
        gain, cure_gain = call(
            rates_kernel,
            "rates",
            (temper, cure, tips),
            [vmem, vmem, anywhere],
            [f32(NX, NY, NZ)] * 2,
            flops=int(1e9),
        )
        if not last:
            tips, own, keep_z = call(
                functools.partial(chain_kernel, 4, DATA_X, ("gx", 0, 3)),
                "chain_z",
                ring,
                [vmem] * 4,
                [f32(2, ROWS_X, NZ), f32(2, ROWS_X, NZ), f32(32, NZ)],
                chain_scratch(4, ROWS_X),
            )
            responses = own
        else:
            *tips, own, passed = call(
                known_z_kernel,
                "chain_z",
                (*ring, keep_z, keep_y, gain),
                [vmem] * 6 + [anywhere],
                [f32(NY, NZ)] * 3 + [f32(2, NY, NZ)] * 2,
                chain_scratch(4, NY),
            )
        ring = exchange(tips, "gx", 4, along_y)
        if not last:
            table, spikes, second_matrix, thick = call(
                prepare_kernel,
                "prepare",
                (
                    inverse_first,
                    conduct_first,
                    inverse_second,
                    conduct_second,
                    inverse_second,
                    conduct_thick,
                    own,
                ),
                (*[smem] * 4, *[vmem] * 2, anywhere),
                [f32(8, NX, NZ), f32(2, NY, NZ), bf16(NY, 3 * NY), f32(8, NZ)],
            )
        (second_done,) = call(
            solve_y_kernel,
            "solve_y",
            (through, second_matrix, own),
            [vmem, vmem, anywhere],
            [f32(NX, NY, NZ)],
            flops=int(1.6e9),
        )
        solved, residual, second_tips = call(
            solve_x_kernel,
            "solve_x",
            (second_done, through, table),
            [vmem] * 3,
            [f32(NX, NY, NZ), f32(NX, NY, NZ), f32(2, NX, NZ)],
            [pltpu.VMEM((NX, 16, NZ), jnp.float32)] * 2,
            flops=int(1e9),
        )
        outs = [f32(2, ROWS_Y, NZ), f32(2, NY, NZ), f32(2, NY, NZ)]
        known = (passed, own, responses, keep_y) if last else (own,)
        operands = (*ring, *known, thick_high, thick_low, second_matrix, second_tips, table, spikes)
        message, halo_through, halo_second, *more = call(
            functools.partial(middle_kernel, last),
            "middle",
            operands,
            [vmem] * len(operands),
            outs if last else outs + [f32(32, NZ)],
            ([pltpu.VMEM((4, NY, NZ), jnp.float32)] * 4 if last else chain_scratch(4, ROWS_X))
            + [pltpu.VMEM((2, NY, NZ), jnp.float32)],
        )
        if not last:
            (keep_y,) = more
        pair = exchange(message, "gy", 2, along_core)
        if last:
            *message, own, passed = call(
                known_core_kernel,
                "chain_core",
                (*pair, keep_x),
                [vmem] * 3,
                [f32(ROWS_Y, NZ)] * 3 + [f32(2, ROWS_Y, NZ)] * 2,
                chain_scratch(2, ROWS_Y),
            )
        else:
            message, own = call(
                functools.partial(chain_kernel, 2, DATA_Y, ("gy", 0, 1)),
                "chain_core",
                pair,
                [vmem] * 2,
                [f32(2, ROWS_Y, NZ)] * 2,
                chain_scratch(2, ROWS_Y),
            )
        ring = exchange(message, "gy", 4, along_x)
        if last:
            ring = [*ring, passed, keep_x]
        base, cure_base = call(
            local_kernel,
            "local",
            (solved, residual, temp, cure_adj, gain, cure_gain, halo_second, halo_through, table, thick),
            [vmem] * 10,
            [f32(NX, NY, NZ)] * 2,
            flops=int(1.6e9),
            limit=20 * MIB,
        )
        outs = [f32(NX, NY, NZ)] * 2 + ([] if last else [f32(2, NY, NZ), f32(32, NZ)])
        buffers = [pltpu.VMEM((4, NX, 16, NZ), jnp.float32)] * 2 + [pltpu.SemaphoreType.DMA((4, 2))]
        results = call(
            functools.partial(final_kernel, last),
            "final",
            (*ring, own, base, gain, cure_base, cure_gain, spikes, table, thick),
            [vmem] * (13 if last else 12),
            outs,
            ([pltpu.VMEM((4, ROWS_Y, NZ), jnp.float32)] * 4 if last else chain_scratch(4, ROWS_Y))
            + [pltpu.VMEM((2, 48, NZ), jnp.float32), pltpu.VMEM((2, NX, NZ), jnp.float32)]
            + (buffers if last else []),
            limit=20 * MIB,
            out_space=pl.BlockSpec(memory_space=pl.ANY) if last else vmem,
        )
        temp, cure_adj = results[0], results[1]
        if not last:
            tips, keep_x = results[2:]
    return (temp, cure_adj)


def solution(mesh):
    placed = (
        P("gx", "gy", None),
        P("gx", "gy", None),
        P("gx", "gy", None),
        P("gx", "gy", None),
        P("gx", "gy", None),
        P("gx", "gy", None),
        P("gx"),
        P("gx", None),
        P("gy"),
        P("gy", None),
        P(),
        P(),
    )
    return jax.shard_map(
        per_device,
        mesh=mesh,
        in_specs=placed,
        out_specs=(P("gx", "gy", None), P("gx", "gy", None)),
        check_vma=False,
    )
```

```python
import functools

import jax
import jax.numpy as jnp
from jax import lax
from jax.experimental import pallas as pl
from jax.experimental.pallas import tpu as pltpu
from jax.sharding import PartitionSpec as P

explicit_part = 2.0
heat_release = 100.0
cure_step = 0.5
arrhenius = 0.5
initial_rate = 0.1
highest = lax.Precision.HIGHEST

NX, NY, NZ = 32, 64, 256
ROWS_X, ROWS_Y = 72, 40
PACKED = 136
MASKS, LISTED = (2, 3, 1), (1, 3, 2)
DATA_X, DATA_Y = 64, 34
MIB = 1024 * 1024


vmem = pl.BlockSpec(memory_space=pltpu.VMEM)
smem = pl.BlockSpec(memory_space=pltpu.SMEM)
anywhere = pl.BlockSpec(memory_space=pl.ANY)


def f32(*shape):
    return jax.ShapeDtypeStruct(shape, jnp.float32)


def bf16(*shape):
    return jax.ShapeDtypeStruct(shape, jnp.bfloat16)


def call(kernel, name, operands, in_specs, outs, scratch=(), flops=0, limit=12 * MIB, out_space=vmem):
    size = sum(x.size * 4 for x in operands) + sum(o.size * 4 for o in outs)
    return pl.pallas_call(
        kernel,
        name=name,
        out_shape=tuple(outs),
        in_specs=list(in_specs),
        out_specs=tuple([out_space] * len(outs)),
        scratch_shapes=list(scratch),
        compiler_params=pltpu.CompilerParams(vmem_limit_bytes=limit),
        cost_estimate=pl.CostEstimate(flops=flops, bytes_accessed=size, transcendentals=0),
    )(*operands)


def place_on(axis, low, mask):
    return lax.bitwise_and(lax.shift_right_logical(lax.axis_index(axis), low), mask)


def chain(count, place, parts, data, gather, alphas, betas, keep=None):
    rows = gather.shape[2]
    masks = (0, 1) if count == 2 else (0, *MASKS)
    for mask, part in zip(masks, parts):
        spot = lax.bitwise_xor(place, mask)
        if len(part.shape) == 3:
            gather[spot] = part[...]
            continue
        gather[spot, 0, :DATA_X, :] = part[:DATA_X, :]
        gather[spot, 1, :DATA_X, :] = part[DATA_X : 2 * DATA_X, :]
        gather[spot, 0, DATA_X:, :] = part[2 * DATA_X :, :]
        gather[spot, 1, DATA_X : DATA_X + 2, :] = part[2 * DATA_X + 2 : 2 * DATA_X + 4, :]
        gather[spot, 1, DATA_X + 2 :, :] = jnp.zeros((6, NZ), jnp.float32)
    row = lax.broadcasted_iota(jnp.int32, (rows, NZ), 0)
    is_left, is_right = row == data, row == data + 1

    def source(j, end):
        value = gather[j, end]
        if j != 0:
            value = jnp.where(is_left, 0.0, value)
        if j != count - 1:
            value = jnp.where(is_right, 0.0, value)
        return value

    def coefficient(j, end, side):
        return gather[j, end, data + side : data + side + 1, :]

    first = [source(j, 0) for j in range(count)]
    last = [source(j, 1) for j in range(count)]
    left_first = [coefficient(j, 0, 0) for j in range(count)]
    left_last = [coefficient(j, 1, 0) for j in range(count)]
    right_first = [coefficient(j, 0, 1) for j in range(count)]
    right_last = [coefficient(j, 1, 1) for j in range(count)]

    pre, corner = [last[0]], [right_last[0]]
    forward, backward, both = [jnp.zeros_like(left_first[0])], {count - 1: jnp.zeros_like(left_first[0])}, []
    for t in range(1, count):
        inv = 1.0 / (1.0 - corner[-1] * left_first[t])
        gain = left_last[t] * inv
        forward.append(gain)
        pre.append(last[t] + gain * (pre[-1] + corner[-1] * first[t]))
        corner.append(right_last[t] + gain * corner[-1] * right_first[t])
    post, bend = {count - 1: first[-1]}, {count - 1: left_first[-1]}
    for t in range(count - 2, -1, -1):
        e, g = post[t + 1], bend[t + 1]
        gain = right_first[t] / (1.0 - g * right_last[t])
        backward[t] = gain
        post[t] = first[t] + gain * (e + g * last[t])
        bend[t] = left_first[t] + gain * g * left_last[t]
    alphas[0] = jnp.where(is_left, 1.0, jnp.zeros((rows, NZ), jnp.float32))
    betas[count - 1] = jnp.where(is_right, 1.0, jnp.zeros((rows, NZ), jnp.float32))
    for t in range(count - 1):
        a, c, e, g = pre[t], corner[t], post[t + 1], bend[t + 1]
        inv = 1.0 / (1.0 - c * g)
        alphas[t + 1] = (a + c * e) * inv
        betas[t] = (e + g * a) * inv
        both.append(inv)
    if keep is not None:
        both.append(jnp.zeros_like(both[0]))
        for t in range(count):
            from_right = forward[t] * corner[t - 1] if t else forward[0]
            from_left = backward[t] * bend[t + 1] if t < count - 1 else backward[t]
            rows_of = (corner[t], forward[t], bend[t], backward[t], both[t], from_right, from_left)
            for kind, value in enumerate(rows_of):
                keep[kind * count + t : kind * count + t + 1, :] = value
    return post[0], pre[-1], alphas[place], betas[place]


def kept(keep, kind, t):
    return keep[4 * kind + t : 4 * kind + t + 1, :]


def interfaces(place, pre, post, keep, alphas, betas):
    alphas[0] = jnp.zeros_like(pre[0])
    betas[3] = jnp.zeros_like(pre[0])
    for t in range(3):
        c, g, both = kept(keep, 0, t), kept(keep, 2, t + 1), kept(keep, 4, t)
        alphas[t + 1] = (pre[t] + c * post[t + 1]) * both
        betas[t] = (post[t + 1] + g * pre[t]) * both
    return alphas[place], betas[place]


def known_core_kernel(*refs):
    parts, keep, messages, own, passed = refs[:2], refs[2], refs[3:6], refs[6], refs[7]
    e, a, alpha, beta = chain(2, place_on("gy", 0, 1), parts, DATA_Y, *refs[8:11])
    own[0] = alpha
    own[1] = beta
    pass_on(place_on("gy", 1, 3), e, a, keep, messages, passed)


def known_z_kernel(*refs):
    parts, keep, keep_next = refs[:4], refs[4], refs[5]
    messages, own, passed = refs[7:10], refs[10], refs[11]
    gather, alphas, betas = refs[12:15]
    place = place_on("gx", 0, 3)
    for mask, part in zip((0, *MASKS), parts):
        gather[lax.bitwise_xor(place, mask)] = part[...]
    first = [gather[j, 0] for j in range(4)]
    last = [gather[j, 1] for j in range(4)]
    pre, post = [last[0]], {3: first[3]}
    for t in range(1, 4):
        c, d = kept(keep, 0, t - 1), kept(keep, 1, t)
        pre.append(last[t] + d * (pre[-1] + c * first[t]))
    for t in range(2, -1, -1):
        g, e = kept(keep, 2, t + 1), kept(keep, 3, t)
        post[t] = first[t] + e * (post[t + 1] + g * last[t])
    alpha, beta = interfaces(place, pre, post, keep, alphas, betas)
    own[0] = alpha
    own[1] = beta
    pass_on(place_on("gx", 2, 3), post[0], pre[3], keep_next, messages, passed)


def pass_on(line, first, last, keep, messages, passed):
    upwards = last + keep[pl.ds(20 + line, 1), :] * first
    downwards = first + keep[pl.ds(24 + line, 1), :] * last
    passed[0] = upwards
    passed[1] = downwards
    for mask, message in zip(LISTED, messages):
        message[...] = jnp.where(lax.bitwise_xor(line, mask) > line, upwards, downwards)


def known_line(line, parts, passed, keep, ups, downs, alphas, betas):
    for mask, part in zip(LISTED, parts):
        place = lax.bitwise_xor(line, mask)
        value = part[...]
        ups[place] = value
        downs[place] = value
    ups[line] = passed[0]
    downs[line] = passed[1]
    pre, post = [ups[0]], {3: downs[3]}
    for t in range(1, 4):
        pre.append(ups[t] + kept(keep, 1, t) * pre[-1])
    for t in range(2, -1, -1):
        post[t] = downs[t] + kept(keep, 3, t) * post[t + 1]
    return interfaces(line, pre, post, keep, alphas, betas)


def chain_scratch(count, rows):
    return [
        pltpu.VMEM((count, 2, rows, NZ), jnp.float32),
        pltpu.VMEM((count, rows, NZ), jnp.float32),
        pltpu.VMEM((count, rows, NZ), jnp.float32),
    ]


def tips_kernel(field_hbm, inv_hbm, faces_hbm, out, inv, faces, field, sems):
    small = [
        pltpu.make_async_copy(inv_hbm, inv, sems.at[8]),
        pltpu.make_async_copy(faces_hbm, faces, sems.at[9]),
    ]
    large = []
    for block in range(8):
        span = slice(block * 8, block * 8 + 8)
        large.append(
            pltpu.make_async_copy(field_hbm.at[:, span, :], field.at[:, span, :], sems.at[block])
        )
    for copy in small + large:
        copy.start()
    for copy in small:
        copy.wait()
    for block in range(8):
        span = slice(block * 8, block * 8 + 8)
        large[block].wait()
        low = inv[0, 0] * field[0, span, :]
        high = inv[0, NX - 1] * field[0, span, :]
        for i in range(1, NX):
            value = field[i, span, :]
            low = low + inv[i, 0] * value
            high = high + inv[i, NX - 1] * value
        out[span, :] = low
        out[DATA_X + block * 8 : DATA_X + block * 8 + 8, :] = high
    row = lax.broadcasted_iota(jnp.int32, (8, NZ), 0)
    ends = jnp.zeros((8, NZ), jnp.float32)
    for number, (face, i, j) in enumerate(
        ((0, 0, 0), (NX, NX - 1, 0), (0, 0, NX - 1), (NX, NX - 1, NX - 1))
    ):
        ends = jnp.where(row == number, faces[face] * inv[i, j], ends)
    out[2 * DATA_X :, :] = ends


def chain_kernel(count, data, place, *refs):
    parts, (tips, own), scratch = refs[:count], refs[count : count + 2], refs[-3:]
    keep = refs[count + 2] if len(refs) > count + 5 else None
    e, a, alpha, beta = chain(count, place_on(*place), parts, data, *scratch, keep)
    own[0] = alpha
    own[1] = beta
    if len(tips.shape) == 3:
        tips[0] = e
        tips[1] = a
        return
    tips[:DATA_X, :] = e[:DATA_X]
    tips[DATA_X : 2 * DATA_X, :] = a[:DATA_X]
    tips[2 * DATA_X : 2 * DATA_X + 2, :] = e[DATA_X : DATA_X + 2]
    tips[2 * DATA_X + 2 : 2 * DATA_X + 4, :] = a[DATA_X : DATA_X + 2]
    tips[2 * DATA_X + 4 :, :] = jnp.zeros((4, NZ), jnp.float32)


def split(value):
    high = value.astype(jnp.bfloat16)
    return high, (value - high.astype(jnp.float32)).astype(jnp.bfloat16)


def product(left, right):
    return jnp.dot(left, right, preferred_element_type=jnp.float32)


def times_thick(value, thick_high, thick_low):
    high, low = split(value)
    total = product(low, thick_high[...]) + product(high, thick_low[...])
    return total + product(high, thick_high[...])


def times_second(second, value):
    high, low = split(value)
    return product(second[...], jnp.concatenate([high, high, low], axis=0))


def prepare_thick_kernel(inverse_thick, thick_high, thick_low):
    thick_high[...], thick_low[...] = split(inverse_thick[...])


def prepare_kernel(
    inv, faces, inv_second, faces_second, inverse_t, thick, unused,
    table, spikes, second, thick_rows,
):
    def row(value):
        return jnp.full((1, NZ), value, jnp.float32)

    delta = row(1.0 + faces[0] + faces[1])
    for i in range(NX):
        table[0, i : i + 1, :] = row(faces[0] * inv[0, i])
        table[1, i : i + 1, :] = row(faces[NX] * inv[NX - 1, i])
        table[2, i : i + 1, :] = row(faces[i])
        table[3, i : i + 1, :] = row(faces[i + 1])
        table[6, i : i + 1, :] = row(inv[i, 0])
        table[7, i : i + 1, :] = row(inv[i, NX - 1])
        inverse = 1.0 / delta
        table[5, i : i + 1, :] = inverse
        ratio = faces[i + 1] * inverse
        table[4, i : i + 1, :] = ratio
        if i < NX - 1:
            delta = 1.0 + faces[i + 1] + faces[i + 2] - faces[i + 1] * ratio
    for y in range(NY):
        spikes[0, y : y + 1, :] = row(faces_second[0] * inv_second[0, y])
        spikes[1, y : y + 1, :] = row(faces_second[NY] * inv_second[NY - 1, y])
    high, low = split(inverse_t[...].T)
    second[...] = jnp.concatenate([high, low, high], axis=1)
    below = thick[0:NZ].reshape(1, NZ)
    above = thick[1 : NZ + 1].reshape(1, NZ)
    lane = lax.broadcasted_iota(jnp.int32, (1, NZ), 1)
    thick_rows[0:1, :] = below
    thick_rows[1:2, :] = above
    thick_rows[2:3, :] = below + above
    thick_rows[3:4, :] = jnp.where(lane == 0, 0.0, below)
    thick_rows[4:5, :] = jnp.where(lane == NZ - 1, 0.0, above)


def rates_kernel(temper, cure, unused, gain, cure_gain):
    @pl.loop(0, NX, unroll=2)
    def _(i):
        c = cure[i]
        heating = jnp.exp(arrhenius * temper[i])
        remain = 1.0 - c
        heated = heating * remain
        ready = initial_rate + c
        gain[i] = (heat_release * arrhenius) * (heated * ready * remain)
        cure_gain[i] = heat_release * (heated * (remain - 2.0 * ready))


def solve_z_kernel(field, thick_high, thick_low, out):
    @pl.loop(0, 8)
    def _(block):
        span = pl.ds(block * 4, 4)
        value = field[span].reshape(4 * NY, NZ)
        out[span] = times_thick(value, thick_high, thick_low).reshape(4, NY, NZ)


def solve_y_kernel(field, second, unused, out):
    @pl.loop(0, NX, unroll=4)
    def _(i):
        out[i] = times_second(second, field[i])


def solve_x_kernel(second_done, through, table, solved, residual, tips, work, work_through):
    zero = jnp.zeros((16, NZ), jnp.float32)
    for block in range(4):
        span = slice(block * 16, block * 16 + 16)

        def forward(i, carry):
            value, whole, ratio = carry
            value = second_done[i, span, :] + ratio * value
            whole = through[i, span, :] + ratio * whole
            work[i] = value
            work_through[i] = whole
            return value, whole, table[4, pl.ds(i, 1), :]

        lax.fori_loop(0, NX, forward, (zero, zero, jnp.zeros((1, NZ), jnp.float32)), unroll=32)

        def backward(step, carry):
            i = NX - 1 - step
            value, whole = carry
            inverse, ratio = table[5, pl.ds(i, 1), :], table[4, pl.ds(i, 1), :]
            value = inverse * work[i] + ratio * value
            whole = inverse * work_through[i] + ratio * whole
            solved[i, span, :] = value
            residual[i, span, :] = (second_done[i, span, :] - value) + (whole - value)
            if block == 0:
                tips[0, pl.ds(i, 1), :] = value[0:1]
            if block == 3:
                tips[1, pl.ds(i, 1), :] = value[15:16]
            return value, whole

        lax.fori_loop(0, NX, backward, (zero, zero), unroll=32)


def middle_kernel(last, *refs):
    if last:
        parts, passed, own, responses, keep = refs[:3], *refs[3:7]
        rest = refs[7:]
    else:
        parts, own = refs[:4], refs[4]
        responses, rest = own, refs[5:]
    thick_high, thick_low, second_matrix, tips, table, spikes, out, through, second = rest[:9]
    scratch, halo = rest[-4 - last : -1], rest[-1]
    if last:
        p, n = known_line(place_on("gx", 2, 3), parts, passed, keep, *scratch)
    else:
        unused, unused, p, n = chain(4, place_on("gx", 2, 3), parts, DATA_X, *scratch, rest[9])
        p, n = p[:DATA_X], n[:DATA_X]
    for side in range(2):
        halo[side] = (
            own[side, :DATA_X, :]
            + responses[side, DATA_X : DATA_X + 1, :] * p
            + responses[side, DATA_X + 1 : DATA_X + 2, :] * n
        )
    through[...] = times_thick(
        halo[...].reshape(2 * NY, NZ), thick_high, thick_low
    ).reshape(2, NY, NZ)
    for side in range(2):
        second[side] = times_second(second_matrix, through[side])
    for end in range(2):
        y = end * (NY - 1)
        prev_row, next_row = second[0, y : y + 1, :], second[1, y : y + 1, :]
        out[end, :NX, :] = tips[end] + table[0] * prev_row + table[1] * next_row
        row = lax.broadcasted_iota(jnp.int32, (8, NZ), 0)
        left, right = spikes[0, y : y + 1, :], spikes[1, y : y + 1, :]
        out[end, NX:, :] = jnp.where(
            row == 0,
            prev_row,
            jnp.where(row == 1, next_row, jnp.where(row == 2, left, jnp.where(row == 3, right, 0.0))),
        )


def lane_stencil(value, thick):
    lower, upper = pltpu.roll(value, 1, 1), pltpu.roll(value, NZ - 1, 1)
    return thick[2:3, :] * value - thick[3:4, :] * lower - thick[4:5, :] * upper


def local_kernel(
    solved, residual, temp, cure_adj, gain, cure_gain, second, halo_through, table, thick,
    base, cure_base,
):
    for block in range(4):
        span = slice(block * 16, block * 16 + 16)
        prev_value, next_value = second[0, span, :], second[1, span, :]
        prev_rest = halo_through[0, span, :] - 2.0 * prev_value
        next_rest = halo_through[1, span, :] - 2.0 * next_value

        @pl.loop(0, NX, unroll=16)
        def _(i):
            left, right = table[0, pl.ds(i, 1), :], table[1, pl.ds(i, 1), :]
            value = solved[i, span, :] + left * prev_value + right * next_value
            kick = residual[i, span, :] + left * prev_rest + right * next_rest
            kick = kick + lane_stencil(value, thick)
            lc = cure_adj[i, span, :]
            source = value + (cure_step / heat_release) * lc
            base[i, span, :] = temp[i, span, :] - explicit_part * kick + gain[i, span, :] * source
            cure_base[i, span, :] = lc + cure_gain[i, span, :] * source


def final_kernel(last, *refs):
    count = 5 if last else 4
    parts, tail = refs[:count], refs[count:]
    own, base, gain, cure_base, cure_gain, spikes, table, thick, temp_out, cure_out = tail[:10]
    if last:
        scratch, rest = tail[10:14], tail[14:]
        p, n = known_line(place_on("gy", 1, 3), parts[:3], parts[3], parts[4], *scratch)
    else:
        tips, keep = tail[10:12]
        scratch, rest = tail[12:15], tail[15:]
        unused, unused, p, n = chain(4, place_on("gy", 1, 3), parts, DATA_Y, *scratch, keep)
    halo, kicks = rest[:2]
    for side in range(2):
        value = (
            own[side]
            + own[side, DATA_Y : DATA_Y + 1, :] * p
            + own[side, DATA_Y + 1 : DATA_Y + 2, :] * n
        )
        halo[side, 8:40, :] = value[:NX]
        halo[side, 7:8, :] = value[NX : NX + 1]
        halo[side, 40:41, :] = value[NX + 1 : NX + 2]
        here = value[:NX]
        lower, upper = halo[side, 7:39, :], halo[side, 9:41, :]
        kick = table[2] * (here - lower) + table[3] * (here - upper)
        kicks[side] = -explicit_part * (kick + lane_stencil(here, thick))
    if last:
        temp_buffer, cure_buffer, sems = rest[2:5]
    copies = []
    for block in range(4):
        span = slice(block * 16, block * 16 + 16)
        left, right = spikes[0, span, :], spikes[1, span, :]

        def step(i, carry):
            delta = left * halo[0, pl.ds(i + 8, 1), :] + right * halo[1, pl.ds(i + 8, 1), :]
            kick = left * kicks[0, pl.ds(i, 1), :] + right * kicks[1, pl.ds(i, 1), :]
            value = base[i, span, :] + (gain[i, span, :] + explicit_part) * delta + kick
            cure_value = cure_base[i, span, :] + cure_gain[i, span, :] * delta
            if last:
                temp_buffer[block, i] = value
                cure_buffer[block, i] = cure_value
                return carry
            temp_out[i, span, :] = value
            cure_out[i, span, :] = cure_value
            low, high = carry
            low = low + table[6, pl.ds(i, 1), :] * value
            return low, high + table[7, pl.ds(i, 1), :] * value

        zero = jnp.zeros((16, NZ), jnp.float32)
        carry = lax.fori_loop(0, NX, step, () if last else (zero, zero), unroll=32)
        if last:
            for buffer, out, sem in (
                (temp_buffer, temp_out, sems.at[block, 0]),
                (cure_buffer, cure_out, sems.at[block, 1]),
            ):
                copy = pltpu.make_async_copy(buffer.at[block], out.at[:, span, :], sem)
                copy.start()
                copies.append(copy)
        else:
            tips[0, span, :] = carry[0]
            tips[1, span, :] = carry[1]
    for copy in copies:
        copy.wait()


def exchange(message, axis, count, index):
    size = lax.axis_size(axis)
    at = {index(device): device for device in range(size)}
    several = isinstance(message, list)
    received = [] if several else [message]
    for number, mask in enumerate((1,) if count == 2 else LISTED if several else MASKS):
        move = [(at[(rest, here)], at[(rest, here ^ mask)]) for rest, here in at]
        received.append(lax.ppermute(message[number] if several else message, axis, move))
    return received


def along_z(device):
    return device // 4, device % 4


def along_y(device):
    return device % 4, device // 4


def along_core(device):
    return device // 2, device % 2


def along_x(device):
    return device % 2, device // 2


def per_device(
    temper_start,
    cure_start,
    temper_middle,
    cure_middle,
    adjoint_temper,
    adjoint_cure,
    conduct_first,
    inverse_first,
    conduct_second,
    inverse_second,
    conduct_thick,
    inverse_thick,
):
    hbm = pl.BlockSpec(memory_space=pltpu.HBM)
    (tips,) = call(
        tips_kernel,
        "tips",
        (adjoint_temper, inverse_first, conduct_first),
        (hbm, hbm, hbm),
        [f32(PACKED, NZ)],
        [
            pltpu.SMEM((NX, NX), jnp.float32),
            pltpu.SMEM((NX + 1,), jnp.float32),
            pltpu.VMEM((NX, NY, NZ), jnp.float32),
            pltpu.SemaphoreType.DMA((10,)),
        ],
        limit=65400000,
    )
    temp, cure_adj = adjoint_temper, adjoint_cure
    thick_high, thick_low = call(
        prepare_thick_kernel,
        "prepare_thick",
        (inverse_thick,),
        (vmem,),
        [bf16(NZ, NZ), bf16(NZ, NZ)],
    )
    fields = ((temper_middle, cure_middle), (temper_start, cure_start))
    for number, (temper, cure) in enumerate(fields):
        last = number == 1
        ring = exchange(tips, "gx", 4, along_z)
        (through,) = call(
            solve_z_kernel,
            "solve_z",
            (temp, thick_high, thick_low),
            [vmem] * 3,
            [f32(NX, NY, NZ)],
            flops=int(1.6e9),
        )
        gain, cure_gain = call(
            rates_kernel,
            "rates",
            (temper, cure, tips),
            [vmem, vmem, anywhere],
            [f32(NX, NY, NZ)] * 2,
            flops=int(1e9),
        )
        if not last:
            tips, own, keep_z = call(
                functools.partial(chain_kernel, 4, DATA_X, ("gx", 0, 3)),
                "chain_z",
                ring,
                [vmem] * 4,
                [f32(PACKED, NZ), f32(2, ROWS_X, NZ), f32(32, NZ)],
                chain_scratch(4, ROWS_X),
            )
            responses = own
        else:
            *tips, own, passed = call(
                known_z_kernel,
                "chain_z",
                (*ring, keep_z, keep_y, gain),
                [vmem] * 6 + [anywhere],
                [f32(NY, NZ)] * 3 + [f32(2, NY, NZ)] * 2,
                chain_scratch(4, NY),
            )
        ring = exchange(tips, "gx", 4, along_y)
        if not last:
            table, spikes, second_matrix, thick = call(
                prepare_kernel,
                "prepare",
                (
                    inverse_first,
                    conduct_first,
                    inverse_second,
                    conduct_second,
                    inverse_second,
                    conduct_thick,
                    own,
                ),
                (*[smem] * 4, *[vmem] * 2, anywhere),
                [f32(8, NX, NZ), f32(2, NY, NZ), bf16(NY, 3 * NY), f32(8, NZ)],
            )
        (second_done,) = call(
            solve_y_kernel,
            "solve_y",
            (through, second_matrix, own),
            [vmem, vmem, anywhere],
            [f32(NX, NY, NZ)],
            flops=int(1.6e9),
        )
        solved, residual, second_tips = call(
            solve_x_kernel,
            "solve_x",
            (second_done, through, table),
            [vmem] * 3,
            [f32(NX, NY, NZ), f32(NX, NY, NZ), f32(2, NX, NZ)],
            [pltpu.VMEM((NX, 16, NZ), jnp.float32)] * 2,
            flops=int(1e9),
        )
        outs = [f32(2, ROWS_Y, NZ), f32(2, NY, NZ), f32(2, NY, NZ)]
        known = (passed, own, responses, keep_y) if last else (own,)
        operands = (*ring, *known, thick_high, thick_low, second_matrix, second_tips, table, spikes)
        message, halo_through, halo_second, *more = call(
            functools.partial(middle_kernel, last),
            "middle",
            operands,
            [vmem] * len(operands),
            outs if last else outs + [f32(32, NZ)],
            ([pltpu.VMEM((4, NY, NZ), jnp.float32)] * 4 if last else chain_scratch(4, ROWS_X))
            + [pltpu.VMEM((2, NY, NZ), jnp.float32)],
        )
        if not last:
            (keep_y,) = more
        pair = exchange(message, "gy", 2, along_core)
        if last:
            *message, own, passed = call(
                known_core_kernel,
                "chain_core",
                (*pair, keep_x),
                [vmem] * 3,
                [f32(ROWS_Y, NZ)] * 3 + [f32(2, ROWS_Y, NZ)] * 2,
                chain_scratch(2, ROWS_Y),
            )
        else:
            message, own = call(
                functools.partial(chain_kernel, 2, DATA_Y, ("gy", 0, 1)),
                "chain_core",
                pair,
                [vmem] * 2,
                [f32(2, ROWS_Y, NZ)] * 2,
                chain_scratch(2, ROWS_Y),
            )
        ring = exchange(message, "gy", 4, along_x)
        if last:
            ring = [*ring, passed, keep_x]
        base, cure_base = call(
            local_kernel,
            "local",
            (solved, residual, temp, cure_adj, gain, cure_gain, halo_second, halo_through, table, thick),
            [vmem] * 10,
            [f32(NX, NY, NZ)] * 2,
            flops=int(1.6e9),
            limit=20 * MIB,
        )
        outs = [f32(NX, NY, NZ)] * 2 + ([] if last else [f32(2, NY, NZ), f32(32, NZ)])
        buffers = [pltpu.VMEM((4, NX, 16, NZ), jnp.float32)] * 2 + [pltpu.SemaphoreType.DMA((4, 2))]
        results = call(
            functools.partial(final_kernel, last),
            "final",
            (*ring, own, base, gain, cure_base, cure_gain, spikes, table, thick),
            [vmem] * (13 if last else 12),
            outs,
            ([pltpu.VMEM((4, ROWS_Y, NZ), jnp.float32)] * 4 if last else chain_scratch(4, ROWS_Y))
            + [pltpu.VMEM((2, 48, NZ), jnp.float32), pltpu.VMEM((2, NX, NZ), jnp.float32)]
            + (buffers if last else []),
            limit=20 * MIB,
            out_space=pl.BlockSpec(memory_space=pl.ANY) if last else vmem,
        )
        temp, cure_adj = results[0], results[1]
        if not last:
            tips, keep_x = results[2:]
    return (temp, cure_adj)


def solution(mesh):
    placed = (
        P("gx", "gy", None),
        P("gx", "gy", None),
        P("gx", "gy", None),
        P("gx", "gy", None),
        P("gx", "gy", None),
        P("gx", "gy", None),
        P("gx"),
        P("gx", None),
        P("gy"),
        P("gy", None),
        P(),
        P(),
    )
    return jax.shard_map(
        per_device,
        mesh=mesh,
        in_specs=placed,
        out_specs=(P("gx", "gy", None), P("gx", "gy", None)),
        check_vma=False,
    )
```
